32 devices in a mesh: row: 16 (over z, y, x), col: 2 (over core).
Axes of the slice: x: 2, y: 2, z: 4, core: 2. Of those that a mesh axis runs over, the one named last changes fastest.
Arguments:
- points: bfloat16 [4096, 128], P(('row', 'col')), may hold values from -128 to 128, as said below
- labels: int32 [4096], P(('row', 'col')), may hold values from 0 to 15
- core: float32 [4096], P(('row', 'col')), may hold values from 600 to 1200
Outputs:
- nearest: float32 [4096], P(('row', 'col'))
- nearest_index: int32 [4096], P(('row', 'col'))
The draws below stay inside these ranges and needn't reach their ends.
Inputs may be any that keep to these rules, and one draw needn't show every extreme that they name: `points`: every entry is a whole number.
All inputs are finite; a program needn't handle non-finite values.
Results may differ from the reference program's by a relative error of at most 0.0003.
Values may be sent and summed in bfloat16 or wider, within the bound.
No kernel may reach another device: no remote copies, remote signals or barrier semaphores. Data moves between devices by JAX's collectives and lax.ppermute only.
A program may use at most 64 MiB of HBM per device.

```python
import math
import jax
import jax.numpy as jnp
from jax import lax

D = 128
COMPONENTS = 16
NPTS = 4096


def draw_points(key, part):
    values = jax.random.randint(jax.random.fold_in(key, 13), (NPTS, D), -128, 129)
    return values.astype(jnp.float32).astype(jnp.bfloat16)


def set_ends(entries, stream_key, least, high):
    longest = entries.shape.index(max(entries.shape))
    spots = []
    for shift in (0, 1):
        where = [jax.random.randint(jax.random.fold_in(stream_key, axis), (), 0, length) for axis, length in enumerate(entries.shape)]
        where[longest] = (where[longest] + shift) % entries.shape[longest]
        spots.append(tuple(where))
    return entries.at[spots[0]].set(least).at[spots[1]].set(high)


def levels(stream_key, dims, shards, low, largest):
    level = 1.0
    for dim, parts in shards:
        steps = jax.random.uniform(jax.random.fold_in(jax.random.fold_in(stream_key, 6), dim), (parts,), jnp.float32, low / len(shards), largest / len(shards))
        level = level * jnp.repeat(jnp.exp(steps), dims[dim] // parts).reshape((-1,) + (1,) * (len(dims) - 1 - dim))
    return level


def setup_inputs(seed: int = 0) -> dict:
    seeds = jax.random.split(jax.random.key(seed), 4)
    return {
        "points": draw_points(jax.random.fold_in(seeds[3], 71), 0),
        "labels": set_ends(jax.random.randint(seeds[1], (NPTS,), 0, COMPONENTS), jax.random.fold_in(seeds[1], 1), 0, COMPONENTS - 1).astype(jnp.int32),
        "core": jnp.clip(jnp.exp(math.log(1200.0) - 0.6931472 * jax.random.uniform(seeds[2], (NPTS,), jnp.float32) ** levels(seeds[2], (NPTS,), ((0, 32),), -0.2, 0.2)), 600.0, 1200.0),
    }


def reference(points, labels, core):
    npts = points.shape[0]
    norms = lax.optimization_barrier(jnp.sum(jnp.square(points.astype(jnp.float32)), axis=1))
    block = math.gcd(npts, 512)
    starts = jnp.arange(npts // block, dtype=jnp.int32) * block

    def one_block(start):
        rows = lax.dynamic_slice_in_dim(points, start, block, 0)
        row_norms = lax.dynamic_slice_in_dim(norms, start, block, 0)
        row_core = lax.dynamic_slice_in_dim(core, start, block, 0)
        row_labels = lax.dynamic_slice_in_dim(labels, start, block, 0)
        gram = jnp.dot(rows, points.T, preferred_element_type=jnp.float32)
        dist = jnp.sqrt(row_norms[:, None] + norms[None, :] - 2.0 * gram)
        reach = jnp.maximum(jnp.maximum(row_core[:, None], core[None, :]), dist)
        reach = jnp.where(row_labels[:, None] == labels[None, :], jnp.inf, reach)
        return (lax.optimization_barrier(jnp.min(reach, axis=1)), jnp.argmin(reach, axis=1).astype(jnp.int32))
    first, where = lax.map(one_block, starts)
    return (first.reshape(npts), where.reshape(npts).astype(jnp.int32))
```

```python
import functools

import jax
import jax.numpy as jnp
from jax import lax
from jax.experimental import pallas as pl
from jax.experimental.pallas import tpu as pltpu
from jax.sharding import PartitionSpec as P


META = 8
SAME = 2.0**30
FAR = 2.0**28
LANES = 128
F32 = jnp.float32
BF16 = jnp.bfloat16
NT = (((1,), (1,)), ((), ()))
TN = (((0,), (0,)), ((), ()))


def is_power_of_two(n):
    return n & (n - 1) == 0


def moved(i, o, n):
    return i ^ o if is_power_of_two(n) else (i + o) % n


def came_from(i, o, n):
    if is_power_of_two(n):
        return lax.bitwise_xor(i, jnp.int32(o)) if not isinstance(o, jax.Array) else lax.bitwise_xor(i, o)
    return lax.rem(i - o + n, n)


def parts_of(v):
    a = v.astype(BF16).astype(F32)
    r = v - a
    b = r.astype(BF16).astype(F32)
    return a, b, r - b


def key_of(core):
    square = core * core
    whole = jnp.floor(square + 0.5)
    return jnp.where(jnp.sqrt(whole) == core, whole, square)


def flat_index(cols):
    return lax.axis_index("row") * cols + lax.axis_index("col")


def pack_kernel(p_ref, label_ref, core_ref, out_ref):
    x = p_ref[...]
    out_ref[0:LANES, :] = x
    xf = x.astype(F32)
    square = xf * xf
    high = square.astype(BF16)
    low = (square - high.astype(F32)).astype(BF16)
    ones = jnp.ones((META, LANES), BF16)
    norm = lax.dot_general(ones, high, NT, preferred_element_type=F32)
    norm = norm + lax.dot_general(ones, low, NT, preferred_element_type=F32)
    core = jnp.broadcast_to(core_ref[...], (META, LANES))
    label = jnp.broadcast_to(label_ref[...].astype(F32), (META, LANES))
    row = lax.broadcasted_iota(jnp.int32, (META, LANES), 0)
    meta = jnp.zeros((META, LANES), F32)
    for k, part in enumerate((*parts_of(norm), *parts_of(core), label)):
        meta = jnp.where(row == k, part, meta)
    both = jnp.concatenate([meta, jnp.zeros((META, LANES), F32)], axis=0)
    out_ref[LANES:, :] = both.astype(BF16)


def join_kernel(cols, own_ref, other_ref, out_ref):
    core = lax.rem(flat_index(cols), 2)
    out_ref[pl.ds(pl.multiple_of(core * LANES, LANES), LANES), :] = own_ref[0:LANES, :]
    out_ref[pl.ds(pl.multiple_of((1 - core) * LANES, LANES), LANES), :] = other_ref[0:LANES, :]
    own = own_ref[LANES:, :].astype(F32)[0:META]
    other = other_ref[LANES:, :].astype(F32)[0:META]
    even = jnp.concatenate([own, other], axis=0)
    odd = jnp.concatenate([other, own], axis=0)
    out_ref[2 * LANES :, :] = jnp.where(core == 0, even, odd).astype(BF16)


def pair_kernel(cols, rb, ca, *refs):
    ops = max(rb, ca) - 1
    own_ref, got, swapped = refs[0], refs[1 : 1 + ops], refs[1 + ops : 1 + 2 * ops]
    outs = refs[1 + 2 * ops : 1 + 2 * ops + rb]
    xl, xr, fl, fr, ck, core_i, t_ref = refs[1 + 2 * ops + rb :]
    me = flat_index(cols)
    core, chip = lax.rem(me, 2), lax.div(me, 2)
    a, b = lax.div(chip, rb), lax.rem(chip, rb)
    row16 = lax.broadcasted_iota(jnp.int32, (16, LANES), 0)
    row8 = lax.broadcasted_iota(jnp.int32, (META, LANES), 0)

    def core_of(m8):
        return jnp.sum(jnp.where((row8 >= 3) & (row8 < 6), m8, 0.0), axis=0, keepdims=True)

    def features(m8, left):
        label = jnp.broadcast_to(m8[6:7], (16, LANES)).astype(jnp.int32)
        same = jnp.where(row16 == label, 1.0 if left else SAME, 0.0)
        padded = jnp.concatenate([m8, jnp.zeros((META, LANES), F32)], axis=0)
        if left:
            rest = jnp.where(row16 < 3, padded, jnp.where(row16 < 6, 1.0, 0.0))
        else:
            moved3 = pltpu.roll(padded, 3, 0)
            rest = jnp.where(row16 < 3, 1.0, jnp.where(row16 < 6, moved3, 0.0))
        return jnp.concatenate([same, rest], axis=0).astype(BF16)

    def put_columns(k, ref):
        xl[k * 2 * LANES : (k + 1) * 2 * LANES, :] = ref[0 : 2 * LANES, :]
        meta = ref[2 * LANES :, :].astype(F32)
        for h in range(2):
            m8 = meta[h * META : (h + 1) * META]
            at = (2 * k + h) * LANES
            fl[:, at : at + LANES] = features(m8, True)
            key = jnp.broadcast_to(key_of(core_of(m8)), (16, LANES))
            p0, p1, p2 = parts_of(key)
            ck[:, at : at + LANES] = jnp.where(
                row16 == 0, p0, jnp.where(row16 == 1, p1, jnp.where(row16 == 2, p2, 0.0))
            ).astype(BF16)

    def put_rows(k, ref, which):
        x = ref[pl.ds(pl.multiple_of(which * LANES, LANES), LANES), :]
        xr[k * LANES : (k + 1) * LANES, :] = (x.astype(F32) * -2.0).astype(BF16)
        meta = ref[2 * LANES :, :].astype(F32)
        m8 = jnp.where(which == 0, meta[0:META], meta[META:])
        fr[:, k * LANES : (k + 1) * LANES] = features(m8, False)
        core_i[0:1, k * LANES : (k + 1) * LANES] = core_of(m8)

    put_columns(0, own_ref)
    put_rows(0, own_ref, core)

    @pl.when(core == 0)
    def _():
        for k in range(1, rb):
            put_rows(k, got[k - 1], 1 - core)
        for k in range(1, ca):
            put_columns(k, swapped[k - 1])

    @pl.when(core == 1)
    def _():
        for k in range(1, rb):
            put_rows(k, swapped[k - 1], 1 - core)
        for k in range(1, ca):
            put_columns(k, got[k - 1])

    width = 2 * LANES
    take = jnp.where(lax.broadcasted_iota(jnp.int32, (16, LANES), 0) < 3, 1.0, 0.0).astype(BF16)

    def groups(v):
        return v.reshape(width // 8, 8, LANES)

    def first_pass(k, best):
        at = pl.multiple_of(k * width, width)
        s = lax.dot_general(xl[pl.ds(at, width), :], xr[...], NT, preferred_element_type=F32)
        s = s + lax.dot_general(fl[:, pl.ds(at, width)], fr[...], TN, preferred_element_type=F32)
        key = lax.dot_general(ck[:, pl.ds(at, width)], take, TN, preferred_element_type=F32)
        out = []
        for r in range(rb):
            t = jnp.maximum(s[:, r * LANES : (r + 1) * LANES], key)
            t_ref[pl.ds(at, width), r * LANES : (r + 1) * LANES] = t
            out.append(jnp.minimum(best[r], jnp.min(groups(t), axis=0)))
        return tuple(out)

    start = tuple(jnp.full((8, LANES), jnp.inf, F32) for _ in range(rb))
    best = lax.fori_loop(0, ca, first_pass, start, unroll=ca <= 4)

    values, limits = [], []
    for r in range(rb):
        least = jnp.min(best[r], axis=0, keepdims=True)
        mine = core_i[0:1, r * LANES : (r + 1) * LANES]
        none = least > FAR
        values.append(jnp.where(none, jnp.inf, jnp.maximum(mine, jnp.sqrt(least))))
        base = jnp.maximum(least, key_of(mine))
        root = jnp.sqrt(base)
        limit = jnp.where(jnp.sqrt(base + 1.0) == root, base + 1.0, base)
        limit = jnp.where(jnp.sqrt(base + 2.0) == root, base + 2.0, limit)
        limits.append(jnp.where(none, jnp.inf, jnp.where(base > 2.0**21, limit, base)))

    step = lax.broadcasted_iota(jnp.int32, (width // 8, 8, LANES), 0) * 8
    step = (step + lax.broadcasted_iota(jnp.int32, (width // 8, 8, LANES), 1)).astype(F32)

    def second_pass(k, place):
        at = pl.multiple_of(k * width, width)
        source = came_from(a, k, ca) * rb + b
        here = step + (source * width).astype(F32)
        out = []
        for r in range(rb):
            t = groups(t_ref[pl.ds(at, width), r * LANES : (r + 1) * LANES])
            found = jnp.where(t <= limits[r][None], here, jnp.inf)
            out.append(jnp.minimum(place[r], jnp.min(found, axis=0)))
        return tuple(out)

    place = lax.fori_loop(0, ca, second_pass, start, unroll=ca <= 4)
    for r in range(rb):
        outs[r][0:1, :] = values[r]
        outs[r][1:2, :] = jnp.min(place[r], axis=0, keepdims=True)


def merge_kernel(*refs):
    ins, (value_ref, place_ref) = refs[:-2], refs[-2:]
    value, place = ins[0][0:1, :], ins[0][1:2, :]
    for ref in ins[1:]:
        v, p = ref[0:1, :], ref[1:2, :]
        take = (v < value) | ((v == value) & (p < place))
        value, place = jnp.where(take, v, value), jnp.where(take, p, place)
    value_ref[...] = value
    place_ref[...] = place.astype(jnp.int32)


def shards(rows, cols, points, labels, core):
    count = points.shape[0]
    devices = rows * cols
    chips = devices // 2
    rb = 1
    while rb * rb * 4 <= chips:
        rb *= 2
    ca = chips // rb
    axes = ("row", "col")
    vmem = pl.BlockSpec(memory_space=pltpu.VMEM)

    def call(kernel, shapes, *args, scratch=(), flops=0):
        single = not isinstance(shapes, (tuple, list))
        return pl.pallas_call(
            kernel,
            out_shape=shapes,
            in_specs=[vmem] * len(args),
            out_specs=vmem if single else [vmem] * len(shapes),
            scratch_shapes=list(scratch),
        )(*args)

    def swap(x):
        return lax.ppermute(x, axes, [(d, d ^ 1) for d in range(devices)])

    def chip_to(chip, plane, line):
        a, b = divmod(chip, rb)
        return moved(a, line, ca) * rb + moved(b, plane, rb)

    own = call(pack_kernel, jax.ShapeDtypeStruct((count + 16, LANES), BF16), points, labels.reshape(1, count), core.reshape(1, count))
    other = swap(own)
    block = call(functools.partial(join_kernel, cols), jax.ShapeDtypeStruct((2 * count + 16, LANES), BF16), own, other)

    ops = max(rb, ca) - 1
    got = []
    for k in range(1, ops + 1):
        plane, line = 1 + (k - 1) % (rb - 1), 1 + (k - 1) % (ca - 1)
        pairs = []
        for chip in range(chips):
            pairs.append((2 * chip, 2 * chip_to(chip, plane, 0)))
            pairs.append((2 * chip + 1, 2 * chip_to(chip, 0, line) + 1))
        got.append(lax.ppermute(block, axes, pairs))
    swapped = [swap(x) for x in got]

    partial = call(
        functools.partial(pair_kernel, cols, rb, ca),
        [jax.ShapeDtypeStruct((8, LANES), F32)] * rb,
        block,
        *got,
        *swapped,
        scratch=(
            pltpu.VMEM((2 * count * ca, LANES), BF16),
            pltpu.VMEM((count * rb, LANES), BF16),
            pltpu.VMEM((32, 2 * count * ca), BF16),
            pltpu.VMEM((32, count * rb), BF16),
            pltpu.VMEM((16, 2 * count * ca), BF16),
            pltpu.VMEM((8, count * rb), F32),
            pltpu.VMEM((2 * count * ca, count * rb), F32),
        ),
    )
    back = [partial[0]]
    for k in range(1, rb):
        pairs = [(d, 2 * chip_to(d // 2, (rb - k) % rb if not is_power_of_two(rb) else k, 0) + (1 - d % 2)) for d in range(devices)]
        back.append(lax.ppermute(partial[k], axes, pairs))
    value, place = call(
        merge_kernel,
        [jax.ShapeDtypeStruct((1, count), F32), jax.ShapeDtypeStruct((1, count), jnp.int32)],
        *back,
    )
    return value.reshape(count), place.reshape(count)


def solution(mesh):
    rows, cols = mesh.shape["row"], mesh.shape["col"]
    return jax.shard_map(
        functools.partial(shards, rows, cols),
        mesh=mesh,
        in_specs=(P(("row", "col"), None), P(("row", "col")), P(("row", "col"))),
        out_specs=(P(("row", "col")), P(("row", "col"))),
        check_vma=False,
    )
```

```python
import functools

import jax
import jax.numpy as jnp
from jax import lax
from jax.experimental import pallas as pl
from jax.experimental.pallas import tpu as pltpu
from jax.sharding import PartitionSpec as P


META = 8
SAME = 2.0**30
FAR = 2.0**28
LANES = 128
F32 = jnp.float32
BF16 = jnp.bfloat16
NT = (((1,), (1,)), ((), ()))
TN = (((0,), (0,)), ((), ()))


def is_power_of_two(n):
    return n & (n - 1) == 0


def moved(i, o, n):
    return i ^ o if is_power_of_two(n) else (i + o) % n


def came_from(i, o, n):
    if is_power_of_two(n):
        return lax.bitwise_xor(i, jnp.int32(o)) if not isinstance(o, jax.Array) else lax.bitwise_xor(i, o)
    return lax.rem(i - o + n, n)


def parts_of(v):
    a = v.astype(BF16).astype(F32)
    r = v - a
    b = r.astype(BF16).astype(F32)
    return a, b, r - b


def key_of(core):
    square = core * core
    whole = jnp.floor(square + 0.5)
    return jnp.where(jnp.sqrt(whole) == core, whole, square)


def flat_index(cols):
    return lax.axis_index("row") * cols + lax.axis_index("col")


def pack_kernel(p_ref, label_ref, core_ref, out_ref):
    x = p_ref[...]
    out_ref[0:LANES, :] = x
    xf = x.astype(F32)
    square = xf * xf
    high = square.astype(BF16)
    low = (square - high.astype(F32)).astype(BF16)
    ones = jnp.ones((META, LANES), BF16)
    norm = lax.dot_general(ones, high, NT, preferred_element_type=F32)
    norm = norm + lax.dot_general(ones, low, NT, preferred_element_type=F32)
    core = jnp.broadcast_to(core_ref[...], (META, LANES))
    label = jnp.broadcast_to(label_ref[...].astype(F32), (META, LANES))
    row = lax.broadcasted_iota(jnp.int32, (META, LANES), 0)
    meta = jnp.zeros((META, LANES), F32)
    for k, part in enumerate((*parts_of(norm), *parts_of(core), label)):
        meta = jnp.where(row == k, part, meta)
    both = jnp.concatenate([meta, jnp.zeros((META, LANES), F32)], axis=0)
    out_ref[LANES:, :] = both.astype(BF16)


def join_kernel(cols, own_ref, other_ref, out_ref):
    core = lax.rem(flat_index(cols), 2)
    out_ref[pl.ds(pl.multiple_of(core * LANES, LANES), LANES), :] = own_ref[0:LANES, :]
    out_ref[pl.ds(pl.multiple_of((1 - core) * LANES, LANES), LANES), :] = other_ref[0:LANES, :]
    own = own_ref[LANES:, :].astype(F32)[0:META]
    other = other_ref[LANES:, :].astype(F32)[0:META]
    even = jnp.concatenate([own, other], axis=0)
    odd = jnp.concatenate([other, own], axis=0)
    out_ref[2 * LANES :, :] = jnp.where(core == 0, even, odd).astype(BF16)


def pair_kernel(cols, rb, ca, *refs):
    ops = max(rb, ca) - 1
    own_ref, got, swapped = refs[0], refs[1 : 1 + ops], refs[1 + ops : 1 + 2 * ops]
    outs = refs[1 + 2 * ops : 1 + 2 * ops + rb]
    xl, xr, fl, fr, ck, core_i, t_ref = refs[1 + 2 * ops + rb :]
    me = flat_index(cols)
    core, chip = lax.rem(me, 2), lax.div(me, 2)
    a, b = lax.div(chip, rb), lax.rem(chip, rb)
    row16 = lax.broadcasted_iota(jnp.int32, (16, LANES), 0)
    row8 = lax.broadcasted_iota(jnp.int32, (META, LANES), 0)

    def core_of(m8):
        return jnp.sum(jnp.where((row8 >= 3) & (row8 < 6), m8, 0.0), axis=0, keepdims=True)

    def features(m8, left):
        label = jnp.broadcast_to(m8[6:7], (16, LANES)).astype(jnp.int32)
        same = jnp.where(row16 == label, 1.0 if left else SAME, 0.0)
        padded = jnp.concatenate([m8, jnp.zeros((META, LANES), F32)], axis=0)
        if left:
            rest = jnp.where(row16 < 3, padded, jnp.where(row16 < 6, 1.0, 0.0))
        else:
            moved3 = pltpu.roll(padded, 3, 0)
            rest = jnp.where(row16 < 3, 1.0, jnp.where(row16 < 6, moved3, 0.0))
        return jnp.concatenate([same, rest], axis=0).astype(BF16)

    def put_columns(k, ref):
        xl[k * 2 * LANES : (k + 1) * 2 * LANES, :] = ref[0 : 2 * LANES, :]
        meta = ref[2 * LANES :, :].astype(F32)
        for h in range(2):
            m8 = meta[h * META : (h + 1) * META]
            at = (2 * k + h) * LANES
            fl[:, at : at + LANES] = features(m8, True)
            key = jnp.broadcast_to(key_of(core_of(m8)), (16, LANES))
            p0, p1, p2 = parts_of(key)
            ck[:, at : at + LANES] = jnp.where(
                row16 == 0, p0, jnp.where(row16 == 1, p1, jnp.where(row16 == 2, p2, 0.0))
            ).astype(BF16)

    def put_rows(k, ref, which):
        x = ref[pl.ds(pl.multiple_of(which * LANES, LANES), LANES), :]
        xr[k * LANES : (k + 1) * LANES, :] = (x.astype(F32) * -2.0).astype(BF16)
        meta = ref[2 * LANES :, :].astype(F32)
        m8 = jnp.where(which == 0, meta[0:META], meta[META:])
        fr[:, k * LANES : (k + 1) * LANES] = features(m8, False)
        core_i[0:1, k * LANES : (k + 1) * LANES] = core_of(m8)

    put_columns(0, own_ref)
    put_rows(0, own_ref, core)

    @pl.when(core == 0)
    def _():
        for k in range(1, rb):
            put_rows(k, got[k - 1], 1 - core)
        for k in range(1, ca):
            put_columns(k, swapped[k - 1])

    @pl.when(core == 1)
    def _():
        for k in range(1, rb):
            put_rows(k, swapped[k - 1], 1 - core)
        for k in range(1, ca):
            put_columns(k, got[k - 1])

    width = 2 * LANES
    take = jnp.where(lax.broadcasted_iota(jnp.int32, (16, LANES), 0) < 3, 1.0, 0.0).astype(BF16)

    def groups(v):
        return v.reshape(width // 8, 8, LANES)

    def first_pass(k, best):
        at = pl.multiple_of(k * width, width)
        s = lax.dot_general(xl[pl.ds(at, width), :], xr[...], NT, preferred_element_type=F32)
        s = s + lax.dot_general(fl[:, pl.ds(at, width)], fr[...], TN, preferred_element_type=F32)
        key = lax.dot_general(ck[:, pl.ds(at, width)], take, TN, preferred_element_type=F32)
        out = []
        for r in range(rb):
            t = jnp.maximum(s[:, r * LANES : (r + 1) * LANES], key)
            t_ref[pl.ds(at, width), r * LANES : (r + 1) * LANES] = t
            out.append(jnp.minimum(best[r], jnp.min(groups(t), axis=0)))
        return tuple(out)

    start = tuple(jnp.full((8, LANES), jnp.inf, F32) for _ in range(rb))
    best = lax.fori_loop(0, ca, first_pass, start, unroll=ca <= 4)

    values, limits = [], []
    for r in range(rb):
        least = jnp.min(best[r], axis=0, keepdims=True)
        mine = core_i[0:1, r * LANES : (r + 1) * LANES]
        none = least > FAR
        values.append(jnp.where(none, jnp.inf, jnp.maximum(mine, jnp.sqrt(least))))
        base = jnp.maximum(least, key_of(mine))
        root = jnp.sqrt(base)
        limit = jnp.where(jnp.sqrt(base + 1.0) == root, base + 1.0, base)
        limit = jnp.where(jnp.sqrt(base + 2.0) == root, base + 2.0, limit)
        limits.append(jnp.where(none, jnp.inf, jnp.where(base > 2.0**21, limit, base)))

    step = lax.broadcasted_iota(jnp.int32, (width // 8, 8, LANES), 0) * 8
    step = (step + lax.broadcasted_iota(jnp.int32, (width // 8, 8, LANES), 1)).astype(F32)

    def second_pass(k, place):
        at = pl.multiple_of(k * width, width)
        source = came_from(a, k, ca) * rb + b
        here = step + (source * width).astype(F32)
        out = []
        for r in range(rb):
            t = groups(t_ref[pl.ds(at, width), r * LANES : (r + 1) * LANES])
            found = jnp.where(t <= limits[r][None], here, jnp.inf)
            out.append(jnp.minimum(place[r], jnp.min(found, axis=0)))
        return tuple(out)

    place = lax.fori_loop(0, ca, second_pass, start, unroll=ca <= 4)
    for r in range(rb):
        outs[r][0:1, :] = values[r]
        outs[r][1:2, :] = jnp.min(place[r], axis=0, keepdims=True)


def merge_kernel(*refs):
    ins, (value_ref, place_ref) = refs[:-2], refs[-2:]
    value, place = ins[0][0:1, :], ins[0][1:2, :]
    for ref in ins[1:]:
        v, p = ref[0:1, :], ref[1:2, :]
        take = (v < value) | ((v == value) & (p < place))
        value, place = jnp.where(take, v, value), jnp.where(take, p, place)
    value_ref[...] = value
    place_ref[...] = place.astype(jnp.int32)


def shards(rows, cols, points, labels, core):
    count = points.shape[0]
    devices = rows * cols
    chips = devices // 2
    rb = 1
    while rb * rb * 4 <= chips:
        rb *= 2
    ca = chips // rb
    axes = ("row", "col")
    vmem = pl.BlockSpec(memory_space=pltpu.VMEM)

    def call(kernel, shapes, *args, scratch=(), grant=4 << 20):
        single = not isinstance(shapes, (tuple, list))
        return pl.pallas_call(
            kernel,
            out_shape=shapes,
            in_specs=[vmem] * len(args),
            out_specs=vmem if single else [vmem] * len(shapes),
            scratch_shapes=list(scratch),
            compiler_params=pltpu.CompilerParams(vmem_limit_bytes=grant),
        )(*args)

    def swap(x):
        return lax.ppermute(x, axes, [(d, d ^ 1) for d in range(devices)])

    def chip_to(chip, plane, line):
        a, b = divmod(chip, rb)
        return moved(a, line, ca) * rb + moved(b, plane, rb)

    own = call(pack_kernel, jax.ShapeDtypeStruct((count + 16, LANES), BF16), points, labels.reshape(1, count), core.reshape(1, count))
    other = swap(own)
    block = call(functools.partial(join_kernel, cols), jax.ShapeDtypeStruct((2 * count + 16, LANES), BF16), own, other)

    ops = max(rb, ca) - 1
    got = []
    for k in range(1, ops + 1):
        plane, line = 1 + (k - 1) % (rb - 1), 1 + (k - 1) % (ca - 1)
        pairs = []
        for chip in range(chips):
            pairs.append((2 * chip, 2 * chip_to(chip, plane, 0)))
            pairs.append((2 * chip + 1, 2 * chip_to(chip, 0, line) + 1))
        got.append(lax.ppermute(block, axes, pairs))
    swapped = [swap(x) for x in got]

    partial = call(
        functools.partial(pair_kernel, cols, rb, ca),
        [jax.ShapeDtypeStruct((8, LANES), F32)] * rb,
        block,
        *got,
        *swapped,
        scratch=(
            pltpu.VMEM((2 * count * ca, LANES), BF16),
            pltpu.VMEM((count * rb, LANES), BF16),
            pltpu.VMEM((32, 2 * count * ca), BF16),
            pltpu.VMEM((32, count * rb), BF16),
            pltpu.VMEM((16, 2 * count * ca), BF16),
            pltpu.VMEM((8, count * rb), F32),
            pltpu.VMEM((2 * count * ca, count * rb), F32),
        ),
        grant=(8 << 20) + 2 * (2 * count * ca) * (count * rb) * 4,
    )
    back = [partial[0]]
    for k in range(1, rb):
        pairs = [(d, 2 * chip_to(d // 2, (rb - k) % rb if not is_power_of_two(rb) else k, 0) + (1 - d % 2)) for d in range(devices)]
        back.append(lax.ppermute(partial[k], axes, pairs))
    value, place = call(
        merge_kernel,
        [jax.ShapeDtypeStruct((1, count), F32), jax.ShapeDtypeStruct((1, count), jnp.int32)],
        *back,
    )
    return value.reshape(count), place.reshape(count)


def solution(mesh):
    rows, cols = mesh.shape["row"], mesh.shape["col"]
    return jax.shard_map(
        functools.partial(shards, rows, cols),
        mesh=mesh,
        in_specs=(P(("row", "col"), None), P(("row", "col")), P(("row", "col"))),
        out_specs=(P(("row", "col")), P(("row", "col"))),
        check_vma=False,
    )
```

```python
import functools

import jax
import jax.numpy as jnp
from jax import lax
from jax.experimental import pallas as pl
from jax.experimental.pallas import tpu as pltpu
from jax.sharding import PartitionSpec as P


META = 8
SAME = 2.0**30
FAR = 2.0**28
LANES = 128
F32 = jnp.float32
BF16 = jnp.bfloat16
NT = (((1,), (1,)), ((), ()))
TN = (((0,), (0,)), ((), ()))


def is_power_of_two(n):
    return n & (n - 1) == 0


def moved(i, o, n):
    return i ^ o if is_power_of_two(n) else (i + o) % n


def came_from(i, o, n):
    if is_power_of_two(n):
        return lax.bitwise_xor(i, jnp.int32(o)) if not isinstance(o, jax.Array) else lax.bitwise_xor(i, o)
    return lax.rem(i - o + n, n)


def parts_of(v):
    a = v.astype(BF16).astype(F32)
    r = v - a
    b = r.astype(BF16).astype(F32)
    return a, b, r - b


def key_of(core):
    square = core * core
    whole = jnp.floor(square + 0.5)
    return jnp.where(jnp.sqrt(whole) == core, whole, square)


def flat_index(cols):
    return lax.axis_index("row") * cols + lax.axis_index("col")


def pack_kernel(p_hbm, label_hbm, core_hbm, out_ref, x_ref, label_ref, core_ref, sems):
    copies = [
        pltpu.make_async_copy(source, target, sems.at[k])
        for k, (source, target) in enumerate(((p_hbm, x_ref), (label_hbm, label_ref), (core_hbm, core_ref)))
    ]
    for copy in copies:
        copy.start()
    for copy in copies:
        copy.wait()
    x = x_ref[...]
    out_ref[0:LANES, :] = x
    xf = x.astype(F32)
    square = xf * xf
    high = square.astype(BF16)
    low = (square - high.astype(F32)).astype(BF16)
    ones = jnp.ones((META, LANES), BF16)
    norm = lax.dot_general(ones, high, NT, preferred_element_type=F32)
    norm = norm + lax.dot_general(ones, low, NT, preferred_element_type=F32)
    core = jnp.broadcast_to(core_ref[...], (META, LANES))
    label = jnp.broadcast_to(label_ref[...].astype(F32), (META, LANES))
    row = lax.broadcasted_iota(jnp.int32, (META, LANES), 0)
    meta = jnp.zeros((META, LANES), F32)
    for k, part in enumerate((*parts_of(norm), *parts_of(core), label)):
        meta = jnp.where(row == k, part, meta)
    both = jnp.concatenate([meta, jnp.zeros((META, LANES), F32)], axis=0)
    out_ref[LANES:, :] = both.astype(BF16)


def join_kernel(cols, own_ref, other_ref, out_ref):
    core = lax.rem(flat_index(cols), 2)
    out_ref[pl.ds(pl.multiple_of(core * LANES, LANES), LANES), :] = own_ref[0:LANES, :]
    out_ref[pl.ds(pl.multiple_of((1 - core) * LANES, LANES), LANES), :] = other_ref[0:LANES, :]
    own = own_ref[LANES:, :].astype(F32)[0:META]
    other = other_ref[LANES:, :].astype(F32)[0:META]
    even = jnp.concatenate([own, other], axis=0)
    odd = jnp.concatenate([other, own], axis=0)
    out_ref[2 * LANES :, :] = jnp.where(core == 0, even, odd).astype(BF16)


def pair_kernel(cols, rb, ca, *refs):
    ops = max(rb, ca) - 1
    own_ref, got, swapped = refs[0], refs[1 : 1 + ops], refs[1 + ops : 1 + 2 * ops]
    outs = refs[1 + 2 * ops : 1 + 2 * ops + rb]
    xl, xr, fl, fr, ck, core_i, t_ref = refs[1 + 2 * ops + rb :]
    me = flat_index(cols)
    core, chip = lax.rem(me, 2), lax.div(me, 2)
    a, b = lax.div(chip, rb), lax.rem(chip, rb)
    row16 = lax.broadcasted_iota(jnp.int32, (16, LANES), 0)
    row8 = lax.broadcasted_iota(jnp.int32, (META, LANES), 0)

    def core_of(m8):
        return jnp.sum(jnp.where((row8 >= 3) & (row8 < 6), m8, 0.0), axis=0, keepdims=True)

    def features(m8, left):
        label = jnp.broadcast_to(m8[6:7], (16, LANES)).astype(jnp.int32)
        same = jnp.where(row16 == label, 1.0 if left else SAME, 0.0)
        padded = jnp.concatenate([m8, jnp.zeros((META, LANES), F32)], axis=0)
        if left:
            rest = jnp.where(row16 < 3, padded, jnp.where(row16 < 6, 1.0, 0.0))
        else:
            moved3 = pltpu.roll(padded, 3, 0)
            rest = jnp.where(row16 < 3, 1.0, jnp.where(row16 < 6, moved3, 0.0))
        return jnp.concatenate([same, rest], axis=0).astype(BF16)

    def put_columns(k, ref):
        xl[k * 2 * LANES : (k + 1) * 2 * LANES, :] = ref[0 : 2 * LANES, :]
        meta = ref[2 * LANES :, :].astype(F32)
        for h in range(2):
            m8 = meta[h * META : (h + 1) * META]
            at = (2 * k + h) * LANES
            fl[:, at : at + LANES] = features(m8, True)
            key = jnp.broadcast_to(key_of(core_of(m8)), (16, LANES))
            p0, p1, p2 = parts_of(key)
            ck[:, at : at + LANES] = jnp.where(
                row16 == 0, p0, jnp.where(row16 == 1, p1, jnp.where(row16 == 2, p2, 0.0))
            ).astype(BF16)

    def put_rows(k, ref, which):
        x = ref[pl.ds(pl.multiple_of(which * LANES, LANES), LANES), :]
        xr[k * LANES : (k + 1) * LANES, :] = (x.astype(F32) * -2.0).astype(BF16)
        meta = ref[2 * LANES :, :].astype(F32)
        m8 = jnp.where(which == 0, meta[0:META], meta[META:])
        fr[:, k * LANES : (k + 1) * LANES] = features(m8, False)
        core_i[0:1, k * LANES : (k + 1) * LANES] = core_of(m8)

    put_columns(0, own_ref)
    put_rows(0, own_ref, core)

    @pl.when(core == 0)
    def _():
        for k in range(1, rb):
            put_rows(k, got[k - 1], 1 - core)
        for k in range(1, ca):
            put_columns(k, swapped[k - 1])

    @pl.when(core == 1)
    def _():
        for k in range(1, rb):
            put_rows(k, swapped[k - 1], 1 - core)
        for k in range(1, ca):
            put_columns(k, got[k - 1])

    width = 2 * LANES
    take = jnp.where(lax.broadcasted_iota(jnp.int32, (16, LANES), 0) < 3, 1.0, 0.0).astype(BF16)

    def groups(v):
        return v.reshape(width // 8, 8, LANES)

    def first_pass(k, best):
        at = pl.multiple_of(k * width, width)
        s = lax.dot_general(xl[pl.ds(at, width), :], xr[...], NT, preferred_element_type=F32)
        s = s + lax.dot_general(fl[:, pl.ds(at, width)], fr[...], TN, preferred_element_type=F32)
        key = lax.dot_general(ck[:, pl.ds(at, width)], take, TN, preferred_element_type=F32)
        out = []
        for r in range(rb):
            t = jnp.maximum(s[:, r * LANES : (r + 1) * LANES], key)
            t_ref[pl.ds(at, width), r * LANES : (r + 1) * LANES] = t
            out.append(jnp.minimum(best[r], jnp.min(groups(t), axis=0)))
        return tuple(out)

    start = tuple(jnp.full((8, LANES), jnp.inf, F32) for _ in range(rb))
    best = lax.fori_loop(0, ca, first_pass, start, unroll=ca <= 4)

    values, limits = [], []
    for r in range(rb):
        least = jnp.min(best[r], axis=0, keepdims=True)
        mine = core_i[0:1, r * LANES : (r + 1) * LANES]
        none = least > FAR
        values.append(jnp.where(none, jnp.inf, jnp.maximum(mine, jnp.sqrt(least))))
        base = jnp.maximum(least, key_of(mine))
        root = jnp.sqrt(base)
        limit = jnp.where(jnp.sqrt(base + 1.0) == root, base + 1.0, base)
        limit = jnp.where(jnp.sqrt(base + 2.0) == root, base + 2.0, limit)
        limits.append(jnp.where(none, jnp.inf, jnp.where(base > 2.0**21, limit, base)))

    step = lax.broadcasted_iota(jnp.int32, (width // 8, 8, LANES), 0) * 8
    step = (step + lax.broadcasted_iota(jnp.int32, (width // 8, 8, LANES), 1)).astype(F32)

    def second_pass(k, place):
        at = pl.multiple_of(k * width, width)
        source = came_from(a, k, ca) * rb + b
        here = step + (source * width).astype(F32)
        out = []
        for r in range(rb):
            t = groups(t_ref[pl.ds(at, width), r * LANES : (r + 1) * LANES])
            found = jnp.where(t <= limits[r][None], here, jnp.inf)
            out.append(jnp.minimum(place[r], jnp.min(found, axis=0)))
        return tuple(out)

    place = lax.fori_loop(0, ca, second_pass, start, unroll=ca <= 4)
    for r in range(rb):
        outs[r][0:1, :] = values[r]
        outs[r][1:2, :] = jnp.min(place[r], axis=0, keepdims=True)


def merge_kernel(*refs):
    ins, (value_ref, place_ref) = refs[:-2], refs[-2:]
    value, place = ins[0][0:1, :], ins[0][1:2, :]
    for ref in ins[1:]:
        v, p = ref[0:1, :], ref[1:2, :]
        take = (v < value) | ((v == value) & (p < place))
        value, place = jnp.where(take, v, value), jnp.where(take, p, place)
    value_ref[...] = value
    place_ref[...] = place.astype(jnp.int32)


def shards(rows, cols, points, labels, core):
    count = points.shape[0]
    devices = rows * cols
    chips = devices // 2
    rb = 1
    while rb * rb * 4 <= chips:
        rb *= 2
    ca = chips // rb
    axes = ("row", "col")
    vmem = pl.BlockSpec(memory_space=pltpu.VMEM)

    def call(kernel, shapes, *args, scratch=(), grant=4 << 20, space=pltpu.VMEM):
        single = not isinstance(shapes, (tuple, list))
        return pl.pallas_call(
            kernel,
            out_shape=shapes,
            in_specs=[pl.BlockSpec(memory_space=space)] * len(args),
            out_specs=vmem if single else [vmem] * len(shapes),
            scratch_shapes=list(scratch),
            compiler_params=pltpu.CompilerParams(vmem_limit_bytes=grant),
        )(*args)

    def swap(x):
        return lax.ppermute(x, axes, [(d, d ^ 1) for d in range(devices)])

    def chip_to(chip, plane, line):
        a, b = divmod(chip, rb)
        return moved(a, line, ca) * rb + moved(b, plane, rb)

    inputs = (points, labels.reshape(1, count), core.reshape(1, count))
    own = call(
        pack_kernel,
        jax.ShapeDtypeStruct((count + 2 * META, LANES), BF16),
        *(pltpu.with_memory_space_constraint(x, pltpu.HBM) for x in inputs),
        space=pltpu.HBM,
        scratch=[pltpu.VMEM(x.shape, x.dtype) for x in inputs] + [pltpu.SemaphoreType.DMA((len(inputs),))],
    )
    block = call(
        functools.partial(join_kernel, cols),
        jax.ShapeDtypeStruct((2 * count + 2 * META, LANES), BF16),
        own,
        swap(own),
    )

    ops = max(rb, ca) - 1
    got = []
    for k in range(1, ops + 1):
        plane, line = 1 + (k - 1) % (rb - 1), 1 + (k - 1) % (ca - 1)
        pairs = []
        for chip in range(chips):
            pairs.append((2 * chip, 2 * chip_to(chip, plane, 0)))
            pairs.append((2 * chip + 1, 2 * chip_to(chip, 0, line) + 1))
        got.append(lax.ppermute(block, axes, pairs))
    swapped = [swap(x) for x in got]

    partial = call(
        functools.partial(pair_kernel, cols, rb, ca),
        [jax.ShapeDtypeStruct((8, LANES), F32)] * rb,
        block,
        *got,
        *swapped,
        scratch=(
            pltpu.VMEM((2 * count * ca, LANES), BF16),
            pltpu.VMEM((count * rb, LANES), BF16),
            pltpu.VMEM((32, 2 * count * ca), BF16),
            pltpu.VMEM((32, count * rb), BF16),
            pltpu.VMEM((16, 2 * count * ca), BF16),
            pltpu.VMEM((8, count * rb), F32),
            pltpu.VMEM((2 * count * ca, count * rb), F32),
        ),
        grant=(8 << 20) + 2 * (2 * count * ca) * (count * rb) * 4,
    )
    back = [partial[0]]
    for k in range(rb - 1, 0, -1):
        pairs = [(d, 2 * chip_to(d // 2, k, 0) + 1 - d % 2) for d in range(devices)]
        back.append(lax.ppermute(partial[k], axes, pairs))
    value, place = call(
        merge_kernel,
        [jax.ShapeDtypeStruct((1, count), F32), jax.ShapeDtypeStruct((1, count), jnp.int32)],
        *back,
    )
    return value.reshape(count), place.reshape(count)


def solution(mesh):
    rows, cols = mesh.shape["row"], mesh.shape["col"]
    return jax.shard_map(
        functools.partial(shards, rows, cols),
        mesh=mesh,
        in_specs=(P(("row", "col"), None), P(("row", "col")), P(("row", "col"))),
        out_specs=(P(("row", "col")), P(("row", "col"))),
        check_vma=False,
    )
```

```python
import functools

import jax
import jax.numpy as jnp
from jax import lax
from jax.experimental import pallas as pl
from jax.experimental.pallas import tpu as pltpu
from jax.sharding import PartitionSpec as P


META = 8
SAME = 2.0**30
FAR = 2.0**28
LANES = 128
F32 = jnp.float32
BF16 = jnp.bfloat16
NT = (((1,), (1,)), ((), ()))
TN = (((0,), (0,)), ((), ()))


def is_power_of_two(n):
    return n & (n - 1) == 0


def moved(i, o, n):
    return i ^ o if is_power_of_two(n) else (i + o) % n


def order_of(ops):
    return [2, 1, *range(3, ops + 1)]


def came_from(i, o, n):
    if is_power_of_two(n):
        return lax.bitwise_xor(i, jnp.int32(o)) if not isinstance(o, jax.Array) else lax.bitwise_xor(i, o)
    return lax.rem(i - o + n, n)


def parts_of(v):
    a = v.astype(BF16).astype(F32)
    r = v - a
    b = r.astype(BF16).astype(F32)
    return a, b, r - b


def root_of(x):
    v = jnp.sqrt(x)
    high = v.astype(BF16).astype(F32)
    low = v - high
    left = ((x - high * high) - 2.0 * high * low) - low * low
    return jnp.where(x > 0.0, v + left * (0.5 / v), 0.0)


def key_of(core):
    square = core * core
    whole = jnp.floor(square + 0.5)
    return jnp.where(root_of(whole) == core, whole, square)


def flat_index(cols):
    return lax.axis_index("row") * cols + lax.axis_index("col")


def pack_kernel(p_hbm, label_hbm, core_hbm, out_ref, x_ref, label_ref, core_ref, sems):
    copies = [
        pltpu.make_async_copy(source, target, sems.at[k])
        for k, (source, target) in enumerate(((p_hbm, x_ref), (label_hbm, label_ref), (core_hbm, core_ref)))
    ]
    for copy in copies:
        copy.start()
    for copy in copies:
        copy.wait()
    x = x_ref[...]
    out_ref[0:LANES, :] = x
    xf = x.astype(F32)
    square = xf * xf
    high = square.astype(BF16)
    low = (square - high.astype(F32)).astype(BF16)
    ones = jnp.ones((META, LANES), BF16)
    norm = lax.dot_general(ones, high, NT, preferred_element_type=F32)
    norm = norm + lax.dot_general(ones, low, NT, preferred_element_type=F32)
    core = jnp.broadcast_to(core_ref[...], (META, LANES))
    label = jnp.broadcast_to(label_ref[...].astype(F32), (META, LANES))
    row = lax.broadcasted_iota(jnp.int32, (META, LANES), 0)
    meta = jnp.zeros((META, LANES), F32)
    for k, part in enumerate((*parts_of(norm), *parts_of(core), label)):
        meta = jnp.where(row == k, part, meta)
    both = jnp.concatenate([meta, jnp.zeros((META, LANES), F32)], axis=0)
    out_ref[LANES:, :] = both.astype(BF16)


def join_kernel(cols, own_ref, other_ref, out_ref):
    core = lax.rem(flat_index(cols), 2)
    out_ref[pl.ds(pl.multiple_of(core * LANES, LANES), LANES), :] = own_ref[0:LANES, :]
    out_ref[pl.ds(pl.multiple_of((1 - core) * LANES, LANES), LANES), :] = other_ref[0:LANES, :]
    own = own_ref[LANES:, :].astype(F32)[0:META]
    other = other_ref[LANES:, :].astype(F32)[0:META]
    even = jnp.concatenate([own, other], axis=0)
    odd = jnp.concatenate([other, own], axis=0)
    out_ref[2 * LANES :, :] = jnp.where(core == 0, even, odd).astype(BF16)


def pair_kernel(cols, rb, ca, *refs):
    ops = max(rb, ca) - 1
    own_ref = refs[0]
    got = dict(zip(order_of(ops), refs[1 : 1 + ops]))
    swapped = dict(zip(order_of(ops), refs[1 + ops : 1 + 2 * ops]))
    outs = refs[1 + 2 * ops : 1 + 2 * ops + rb]
    xl, xr, fl, fr, ck, core_i, t_ref = refs[1 + 2 * ops + rb :]
    me = flat_index(cols)
    core, chip = lax.rem(me, 2), lax.div(me, 2)
    a, b = lax.div(chip, rb), lax.rem(chip, rb)
    row16 = lax.broadcasted_iota(jnp.int32, (16, LANES), 0)
    row8 = lax.broadcasted_iota(jnp.int32, (META, LANES), 0)

    def core_of(m8):
        return jnp.sum(jnp.where((row8 >= 3) & (row8 < 6), m8, 0.0), axis=0, keepdims=True)

    def features(m8, left):
        label = jnp.broadcast_to(m8[6:7], (16, LANES)).astype(jnp.int32)
        same = jnp.where(row16 == label, 1.0 if left else SAME, 0.0)
        padded = jnp.concatenate([m8, jnp.zeros((META, LANES), F32)], axis=0)
        if left:
            rest = jnp.where(row16 < 3, padded, jnp.where(row16 < 6, 1.0, 0.0))
        else:
            moved3 = pltpu.roll(padded, 3, 0)
            rest = jnp.where(row16 < 3, 1.0, jnp.where(row16 < 6, moved3, 0.0))
        return jnp.concatenate([same, rest], axis=0).astype(BF16)

    def put_columns(k, ref):
        xl[k * 2 * LANES : (k + 1) * 2 * LANES, :] = ref[0 : 2 * LANES, :]
        meta = ref[2 * LANES :, :].astype(F32)
        for h in range(2):
            m8 = meta[h * META : (h + 1) * META]
            at = (2 * k + h) * LANES
            fl[:, at : at + LANES] = features(m8, True)
            key = jnp.broadcast_to(key_of(core_of(m8)), (16, LANES))
            p0, p1, p2 = parts_of(key)
            ck[:, at : at + LANES] = jnp.where(
                row16 == 0, p0, jnp.where(row16 == 1, p1, jnp.where(row16 == 2, p2, 0.0))
            ).astype(BF16)

    def put_rows(k, ref, which):
        x = ref[pl.ds(pl.multiple_of(which * LANES, LANES), LANES), :]
        xr[k * LANES : (k + 1) * LANES, :] = (x.astype(F32) * -2.0).astype(BF16)
        meta = ref[2 * LANES :, :].astype(F32)
        m8 = jnp.where(which == 0, meta[0:META], meta[META:])
        fr[:, k * LANES : (k + 1) * LANES] = features(m8, False)
        core_i[0:1, k * LANES : (k + 1) * LANES] = core_of(m8)

    put_columns(0, own_ref)
    put_rows(0, own_ref, core)

    @pl.when(core == 0)
    def _():
        for k in range(1, rb):
            put_rows(k, got[k], 1 - core)
        for k in range(1, ca):
            put_columns(k, swapped[k])

    @pl.when(core == 1)
    def _():
        for k in range(1, rb):
            put_rows(k, swapped[k], 1 - core)
        for k in range(1, ca):
            put_columns(k, got[k])

    width = 2 * LANES
    take = jnp.where(lax.broadcasted_iota(jnp.int32, (16, LANES), 0) < 3, 1.0, 0.0).astype(BF16)

    def groups(v):
        return v.reshape(width // 8, 8, LANES)

    def first_pass(k, best):
        at = pl.multiple_of(k * width, width)
        s = lax.dot_general(xl[pl.ds(at, width), :], xr[...], NT, preferred_element_type=F32)
        s = s + lax.dot_general(fl[:, pl.ds(at, width)], fr[...], TN, preferred_element_type=F32)
        key = lax.dot_general(ck[:, pl.ds(at, width)], take, TN, preferred_element_type=F32)
        out = []
        for r in range(rb):
            t = jnp.maximum(s[:, r * LANES : (r + 1) * LANES], key)
            t_ref[pl.ds(at, width), r * LANES : (r + 1) * LANES] = t
            out.append(jnp.minimum(best[r], jnp.min(groups(t), axis=0)))
        return tuple(out)

    start = tuple(jnp.full((8, LANES), jnp.inf, F32) for _ in range(rb))
    best = lax.fori_loop(0, ca, first_pass, start, unroll=ca <= 4)

    values, limits = [], []
    for r in range(rb):
        least = jnp.min(best[r], axis=0, keepdims=True)
        mine = core_i[0:1, r * LANES : (r + 1) * LANES]
        none = least > FAR
        root = root_of(least)
        values.append(jnp.where(none, jnp.inf, jnp.maximum(mine, root)))
        base = jnp.maximum(least, key_of(mine))
        limit = jnp.where(root_of(least + 1.0) == root, least + 1.0, least)
        limit = jnp.where(root_of(least + 2.0) == root, least + 2.0, limit)
        limits.append(jnp.where(none, jnp.inf, jnp.where(least > 2.0**21, limit, base)))

    step = lax.broadcasted_iota(jnp.int32, (width // 8, 8, LANES), 0) * 8
    step = (step + lax.broadcasted_iota(jnp.int32, (width // 8, 8, LANES), 1)).astype(F32)

    def second_pass(k, place):
        at = pl.multiple_of(k * width, width)
        source = came_from(a, k, ca) * rb + b
        here = step + (source * width).astype(F32)
        out = []
        for r in range(rb):
            t = groups(t_ref[pl.ds(at, width), r * LANES : (r + 1) * LANES])
            found = jnp.where(t <= limits[r][None], here, jnp.inf)
            out.append(jnp.minimum(place[r], jnp.min(found, axis=0)))
        return tuple(out)

    place = lax.fori_loop(0, ca, second_pass, start, unroll=ca <= 4)
    for r in range(rb):
        outs[r][0:1, :] = values[r]
        outs[r][1:2, :] = jnp.min(place[r], axis=0, keepdims=True)


def merge_kernel(*refs):
    ins, (value_ref, place_ref) = refs[:-2], refs[-2:]
    value, place = ins[0][0:1, :], ins[0][1:2, :]
    for ref in ins[1:]:
        v, p = ref[0:1, :], ref[1:2, :]
        take = (v < value) | ((v == value) & (p < place))
        value, place = jnp.where(take, v, value), jnp.where(take, p, place)
    value_ref[...] = value
    place_ref[...] = place.astype(jnp.int32)


def shards(rows, cols, points, labels, core):
    count = points.shape[0]
    devices = rows * cols
    chips = devices // 2
    rb = 1
    while rb * rb * 4 <= chips:
        rb *= 2
    ca = chips // rb
    axes = ("row", "col")
    vmem = pl.BlockSpec(memory_space=pltpu.VMEM)

    def call(kernel, shapes, *args, scratch=(), grant=4 << 20, space=pltpu.VMEM):
        single = not isinstance(shapes, (tuple, list))
        return pl.pallas_call(
            kernel,
            out_shape=shapes,
            in_specs=[pl.BlockSpec(memory_space=space)] * len(args),
            out_specs=vmem if single else [vmem] * len(shapes),
            scratch_shapes=list(scratch),
            compiler_params=pltpu.CompilerParams(vmem_limit_bytes=grant),
        )(*args)

    def swap(x):
        return lax.ppermute(x, axes, [(d, d ^ 1) for d in range(devices)])

    def chip_to(chip, plane, line):
        a, b = divmod(chip, rb)
        return moved(a, line, ca) * rb + moved(b, plane, rb)

    inputs = (points, labels.reshape(1, count), core.reshape(1, count))
    own = call(
        pack_kernel,
        jax.ShapeDtypeStruct((count + 2 * META, LANES), BF16),
        *(pltpu.with_memory_space_constraint(x, pltpu.HBM) for x in inputs),
        space=pltpu.HBM,
        scratch=[pltpu.VMEM(x.shape, x.dtype) for x in inputs] + [pltpu.SemaphoreType.DMA((len(inputs),))],
    )
    block = call(
        functools.partial(join_kernel, cols),
        jax.ShapeDtypeStruct((2 * count + 2 * META, LANES), BF16),
        own,
        swap(own),
    )

    ops = max(rb, ca) - 1
    order = order_of(ops)
    got = {}
    for k in order:
        plane, line = 1 + (k - 1) % (rb - 1), 1 + (k - 1) % (ca - 1)
        pairs = []
        for chip in range(chips):
            pairs.append((2 * chip, 2 * chip_to(chip, plane, 0)))
            pairs.append((2 * chip + 1, 2 * chip_to(chip, 0, line) + 1))
        got[k] = lax.ppermute(block, axes, pairs)
    got = [got[k] for k in order]
    swapped = [swap(x) for x in got]

    partial = call(
        functools.partial(pair_kernel, cols, rb, ca),
        [jax.ShapeDtypeStruct((8, LANES), F32)] * rb,
        block,
        *got,
        *swapped,
        scratch=(
            pltpu.VMEM((2 * count * ca, LANES), BF16),
            pltpu.VMEM((count * rb, LANES), BF16),
            pltpu.VMEM((32, 2 * count * ca), BF16),
            pltpu.VMEM((32, count * rb), BF16),
            pltpu.VMEM((16, 2 * count * ca), BF16),
            pltpu.VMEM((8, count * rb), F32),
            pltpu.VMEM((2 * count * ca, count * rb), F32),
        ),
        grant=(8 << 20) + 2 * (2 * count * ca) * (count * rb) * 4,
    )
    back = [partial[0]]
    for k in [1, *range(rb - 1, 1, -1)]:
        pairs = [(d, 2 * chip_to(d // 2, k, 0) + 1 - d % 2) for d in range(devices)]
        back.append(lax.ppermute(partial[k], axes, pairs))
    value, place = call(
        merge_kernel,
        [jax.ShapeDtypeStruct((1, count), F32), jax.ShapeDtypeStruct((1, count), jnp.int32)],
        *back,
    )
    return value.reshape(count), place.reshape(count)


def solution(mesh):
    rows, cols = mesh.shape["row"], mesh.shape["col"]
    return jax.shard_map(
        functools.partial(shards, rows, cols),
        mesh=mesh,
        in_specs=(P(("row", "col"), None), P(("row", "col")), P(("row", "col"))),
        out_specs=(P(("row", "col")), P(("row", "col"))),
        check_vma=False,
    )
```

```python
import functools

import jax
import jax.numpy as jnp
from jax import lax
from jax.experimental import pallas as pl
from jax.experimental.pallas import tpu as pltpu
from jax.sharding import PartitionSpec as P


META = 8
SAME = 2.0**30
FOUR = (3, 2, 0, 1)
FAR = 2.0**28
LANES = 128
F32 = jnp.float32
BF16 = jnp.bfloat16
NT = (((1,), (1,)), ((), ()))
TN = (((0,), (0,)), ((), ()))


def is_power_of_two(n):
    return n & (n - 1) == 0


def moved(i, o, n):
    return i ^ o if is_power_of_two(n) else (i + o) % n


def gather_offsets(rb, ca):
    half = ca // 2
    low = [*range(2, half), 1] if half > 1 else []
    even = [(0, o) for o in low] + [(o, 0) for o in range(1, rb)]
    odd = [(0, half + o) for o in low] + [(0, half)]
    ops = max(len(even), len(odd))
    steps = [(even[k % len(even)], odd[k % len(odd)]) for k in range(ops)]
    return [steps[k] for k in FOUR] if ops == len(FOUR) else steps


def came_from(i, o, n):
    if is_power_of_two(n):
        return lax.bitwise_xor(i, jnp.int32(o)) if not isinstance(o, jax.Array) else lax.bitwise_xor(i, o)
    return lax.rem(i - o + n, n)


def parts_of(v):
    a = v.astype(BF16).astype(F32)
    r = v - a
    b = r.astype(BF16).astype(F32)
    return a, b, r - b


def root_of(x):
    v = jnp.sqrt(x)
    high = v.astype(BF16).astype(F32)
    low = v - high
    left = ((x - high * high) - 2.0 * high * low) - low * low
    return jnp.where(x > 0.0, v + left * (0.5 / v), 0.0)


def key_of(core):
    square = core * core
    whole = jnp.floor(square + 0.5)
    return jnp.where(root_of(whole) == core, whole, square)


def flat_index(cols):
    return lax.axis_index("row") * cols + lax.axis_index("col")


def pack_kernel(p_hbm, label_hbm, core_hbm, out_ref, x_ref, label_ref, core_ref, sems):
    copies = [
        pltpu.make_async_copy(source, target, sems.at[k])
        for k, (source, target) in enumerate(((p_hbm, x_ref), (label_hbm, label_ref), (core_hbm, core_ref)))
    ]
    for copy in copies:
        copy.start()
    for copy in copies:
        copy.wait()
    x = x_ref[...]
    out_ref[0:LANES, :] = x
    xf = x.astype(F32)
    square = xf * xf
    high = square.astype(BF16)
    low = (square - high.astype(F32)).astype(BF16)
    ones = jnp.ones((META, LANES), BF16)
    norm = lax.dot_general(ones, high, NT, preferred_element_type=F32)
    norm = norm + lax.dot_general(ones, low, NT, preferred_element_type=F32)
    core = jnp.broadcast_to(core_ref[...], (META, LANES))
    label = jnp.broadcast_to(label_ref[...].astype(F32), (META, LANES))
    row = lax.broadcasted_iota(jnp.int32, (META, LANES), 0)
    meta = jnp.zeros((META, LANES), F32)
    for k, part in enumerate((*parts_of(norm), *parts_of(core), label)):
        meta = jnp.where(row == k, part, meta)
    both = jnp.concatenate([meta, jnp.zeros((META, LANES), F32)], axis=0)
    out_ref[LANES:, :] = both.astype(BF16)


def join_kernel(cols, own_ref, other_ref, out_ref):
    core = lax.rem(flat_index(cols), 2)
    out_ref[pl.ds(pl.multiple_of(core * LANES, LANES), LANES), :] = own_ref[0:LANES, :]
    out_ref[pl.ds(pl.multiple_of((1 - core) * LANES, LANES), LANES), :] = other_ref[0:LANES, :]
    own = own_ref[LANES:, :].astype(F32)[0:META]
    other = other_ref[LANES:, :].astype(F32)[0:META]
    even = jnp.concatenate([own, other], axis=0)
    odd = jnp.concatenate([other, own], axis=0)
    out_ref[2 * LANES :, :] = jnp.where(core == 0, even, odd).astype(BF16)


def core_of(m8):
    row = lax.broadcasted_iota(jnp.int32, (META, LANES), 0)
    return jnp.sum(jnp.where((row >= 3) & (row < 6), m8, 0.0), axis=0, keepdims=True)


def features(m8, left):
    row = lax.broadcasted_iota(jnp.int32, (2 * META, LANES), 0)
    label = jnp.broadcast_to(m8[6:7], row.shape).astype(jnp.int32)
    same = jnp.where(row == label, 1.0 if left else SAME, 0.0)
    padded = jnp.concatenate([m8, jnp.zeros((META, LANES), F32)], axis=0)
    if left:
        rest = jnp.where(row < 3, padded, jnp.where(row < 6, 1.0, 0.0))
    else:
        rest = jnp.where(row < 3, 1.0, jnp.where(row < 6, pltpu.roll(padded, 3, 0), 0.0))
    return jnp.concatenate([same, rest], axis=0).astype(BF16)


def put_rows(k, ref, which, xr, fr, core_i):
    x = ref[pl.ds(pl.multiple_of(which * LANES, LANES), LANES), :]
    xr[k * LANES : (k + 1) * LANES, :] = (x.astype(F32) * -2.0).astype(BF16)
    meta = ref[2 * LANES :, :].astype(F32)
    m8 = jnp.where(which == 0, meta[0:META], meta[META:])
    fr[:, k * LANES : (k + 1) * LANES] = features(m8, False)
    core_i[0:1, k * LANES : (k + 1) * LANES] = core_of(m8)


def nearest(outs, xl, fl, key_ref, xr, fr, core_i, t_ref, source_of):
    width = 2 * LANES
    blocks, groups_of = len(outs), (width // 8, 8, LANES)
    ca = xl.shape[0] // width

    def first_pass(k, best):
        at = pl.multiple_of(k * width, width)
        s = lax.dot_general(xl[pl.ds(at, width), :], xr[...], NT, preferred_element_type=F32)
        s = s + lax.dot_general(fl[:, pl.ds(at, width)], fr[...], TN, preferred_element_type=F32)
        key = key_ref[pl.ds(at, width), :]
        out = []
        for r in range(blocks):
            t = jnp.maximum(s[:, r * LANES : (r + 1) * LANES], key)
            t_ref[pl.ds(at, width), r * LANES : (r + 1) * LANES] = t
            out.append(jnp.minimum(best[r], jnp.min(t.reshape(groups_of), axis=0)))
        return tuple(out)

    start = tuple(jnp.full((8, LANES), jnp.inf, F32) for _ in outs)
    best = lax.fori_loop(0, ca, first_pass, start, unroll=ca <= 8)

    values, limits = [], []
    for r in range(blocks):
        least = jnp.min(best[r], axis=0, keepdims=True)
        mine = core_i[0:1, r * LANES : (r + 1) * LANES]
        none = least > FAR
        root = root_of(least)
        values.append(jnp.where(none, jnp.inf, jnp.maximum(mine, root)))
        base = jnp.maximum(least, key_of(mine))
        limit = jnp.where(root_of(least + 1.0) == root, least + 1.0, least)
        limit = jnp.where(root_of(least + 2.0) == root, least + 2.0, limit)
        limits.append(jnp.where(none, jnp.inf, jnp.where(least > 2.0**21, limit, base)))

    step = lax.broadcasted_iota(jnp.int32, groups_of, 0) * 8
    step = (step + lax.broadcasted_iota(jnp.int32, groups_of, 1)).astype(F32)

    def second_pass(k, place):
        at = pl.multiple_of(k * width, width)
        here = step + (source_of(k) * width).astype(F32)
        out = []
        for r in range(blocks):
            t = t_ref[pl.ds(at, width), r * LANES : (r + 1) * LANES].reshape(groups_of)
            found = jnp.where(t <= limits[r][None], here, jnp.inf)
            out.append(jnp.minimum(place[r], jnp.min(found, axis=0)))
        return tuple(out)

    place = lax.fori_loop(0, ca, second_pass, start, unroll=ca <= 8)
    for r in range(blocks):
        outs[r][0:1, :] = values[r]
        outs[r][1:2, :] = jnp.min(place[r], axis=0, keepdims=True)


def position(cols, ca):
    me = flat_index(cols)
    chip = lax.div(me, 2)
    return lax.rem(me, 2), lax.div(chip, ca), lax.rem(chip, ca)


def far_kernel(cols, rb, ca, *refs):
    steps = gather_offsets(rb, ca)
    ops = len(steps)
    own_ref, got, swapped = refs[0], refs[1 : 1 + ops], refs[1 + ops : 1 + 2 * ops]
    xl, fl, key_ref, *outs = refs[1 + 2 * ops : 4 + 2 * ops + rb - 1]
    xr, fr, ck, core_i, t_ref = refs[4 + 2 * ops + rb - 1 :]
    core, a, b = position(cols, ca)
    row16 = lax.broadcasted_iota(jnp.int32, (2 * META, LANES), 0)

    def put_columns(k, ref):
        xl[k * 2 * LANES : (k + 1) * 2 * LANES, :] = ref[0 : 2 * LANES, :]
        meta = ref[2 * LANES :, :].astype(F32)
        for h in range(2):
            m8 = meta[h * META : (h + 1) * META]
            at = (2 * k + h) * LANES
            fl[:, at : at + LANES] = features(m8, True)
            key = jnp.broadcast_to(key_of(core_of(m8)), (2 * META, LANES))
            p0, p1, p2 = parts_of(key)
            ck[:, at : at + LANES] = jnp.where(
                row16 == 0, p0, jnp.where(row16 == 1, p1, jnp.where(row16 == 2, p2, 0.0))
            ).astype(BF16)

    put_columns(0, own_ref)

    def put_all(mine):
        seen = set()
        for k, pair in enumerate(steps):
            for side in range(2):
                offset = pair[side]
                if offset in seen:
                    continue
                seen.add(offset)
                ref = got[k] if side == mine else swapped[k]
                if offset[0]:
                    put_rows(offset[0] - 1, ref, 1 - core, xr, fr, core_i)
                else:
                    put_columns(offset[1], ref)

    for side in range(2):
        pl.when(core == side)(functools.partial(put_all, side))

    take = jnp.where(row16 < 3, 1.0, 0.0).astype(BF16)
    key_ref[...] = lax.dot_general(ck[...], take, TN, preferred_element_type=F32)
    nearest(outs, xl, fl, key_ref, xr, fr, core_i, t_ref, lambda k: a * ca + came_from(b, k, ca))


def near_kernel(cols, ca, own_ref, xl, fl, key_ref, out_ref, xr, fr, core_i, t_ref):
    core, a, b = position(cols, ca)
    put_rows(0, own_ref, core, xr, fr, core_i)
    nearest([out_ref], xl, fl, key_ref, xr, fr, core_i, t_ref, lambda k: a * ca + came_from(b, k, ca))


def merge_kernel(*refs):
    ins, (value_ref, place_ref) = refs[:-2], refs[-2:]
    value, place = ins[0][0:1, :], ins[0][1:2, :]
    for ref in ins[1:]:
        v, p = ref[0:1, :], ref[1:2, :]
        take = (v < value) | ((v == value) & (p < place))
        value, place = jnp.where(take, v, value), jnp.where(take, p, place)
    value_ref[...] = value
    place_ref[...] = place.astype(jnp.int32)


def shards(rows, cols, points, labels, core):
    count = points.shape[0]
    devices = rows * cols
    chips = devices // 2
    rb = 1
    while rb * rb * 8 <= chips:
        rb *= 2
    ca = chips // rb
    axes = ("row", "col")
    vmem = pl.BlockSpec(memory_space=pltpu.VMEM)

    def call(kernel, shapes, *args, scratch=(), grant=4 << 20, space=pltpu.VMEM):
        single = not isinstance(shapes, (tuple, list))
        return pl.pallas_call(
            kernel,
            out_shape=shapes,
            in_specs=[pl.BlockSpec(memory_space=space)] * len(args),
            out_specs=vmem if single else [vmem] * len(shapes),
            scratch_shapes=list(scratch),
            compiler_params=pltpu.CompilerParams(vmem_limit_bytes=grant),
        )(*args)

    def swap(x):
        return lax.ppermute(x, axes, [(d, d ^ 1) for d in range(devices)])

    def chip_to(chip, offset):
        a, b = divmod(chip, ca)
        return moved(a, offset[0], rb) * ca + moved(b, offset[1], ca)

    inputs = (points, labels.reshape(1, count), core.reshape(1, count))
    own = call(
        pack_kernel,
        jax.ShapeDtypeStruct((count + 2 * META, LANES), BF16),
        *(pltpu.with_memory_space_constraint(x, pltpu.HBM) for x in inputs),
        space=pltpu.HBM,
        scratch=[pltpu.VMEM(x.shape, x.dtype) for x in inputs] + [pltpu.SemaphoreType.DMA((len(inputs),))],
    )
    block = call(
        functools.partial(join_kernel, cols),
        jax.ShapeDtypeStruct((2 * count + 2 * META, LANES), BF16),
        own,
        swap(own),
    )

    got = []
    for offsets in gather_offsets(rb, ca):
        pairs = [(2 * q + side, 2 * chip_to(q, offsets[side]) + side) for q in range(chips) for side in range(2)]
        got.append(lax.ppermute(block, axes, pairs))
    swapped = [swap(x) for x in got]

    wide, far = 2 * count * ca, count * (rb - 1)
    held = [
        jax.ShapeDtypeStruct((wide, LANES), BF16),
        jax.ShapeDtypeStruct((32, wide), BF16),
        jax.ShapeDtypeStruct((wide, LANES), F32),
    ]
    found = jax.ShapeDtypeStruct((8, LANES), F32)

    def row_scratch(n):
        return [pltpu.VMEM((n, LANES), BF16), pltpu.VMEM((32, n), BF16)], [pltpu.VMEM((8, n), F32), pltpu.VMEM((wide, n), F32)]

    first, last = row_scratch(far)
    results = call(
        functools.partial(far_kernel, cols, rb, ca),
        [*held, *[found] * (rb - 1)],
        block,
        *got,
        *swapped,
        scratch=[*first, pltpu.VMEM((16, wide), BF16), *last],
        grant=(6 << 20) + 2 * wide * far * 4,
    )
    columns, partial = results[:3], results[3:]
    back = []
    for k in range(1, rb):
        pairs = [(d, 2 * chip_to(d // 2, (k, 0)) + 1 - d % 2) for d in range(devices)]
        back.append(lax.ppermute(partial[k - 1], axes, pairs))
    first, last = row_scratch(count)
    own_found = call(
        functools.partial(near_kernel, cols, ca),
        found,
        block,
        *columns,
        scratch=[*first, *last],
        grant=(6 << 20) + 2 * wide * count * 4,
    )
    back.insert(0, own_found)
    value, place = call(
        merge_kernel,
        [jax.ShapeDtypeStruct((1, count), F32), jax.ShapeDtypeStruct((1, count), jnp.int32)],
        *back,
    )
    return value.reshape(count), place.reshape(count)


def solution(mesh):
    rows, cols = mesh.shape["row"], mesh.shape["col"]
    return jax.shard_map(
        functools.partial(shards, rows, cols),
        mesh=mesh,
        in_specs=(P(("row", "col"), None), P(("row", "col")), P(("row", "col"))),
        out_specs=(P(("row", "col")), P(("row", "col"))),
        check_vma=False,
    )
```

```python
import functools

import jax
import jax.numpy as jnp
from jax import lax
from jax.experimental import pallas as pl
from jax.experimental.pallas import tpu as pltpu
from jax.sharding import PartitionSpec as P


META = 8
SAME = 2.0**30
FAR = 2.0**28
LANES = 128
F32 = jnp.float32
BF16 = jnp.bfloat16
NT = (((1,), (1,)), ((), ()))
TN = (((0,), (0,)), ((), ()))


def is_power_of_two(n):
    return n & (n - 1) == 0


def moved(i, o, n):
    return i ^ o if is_power_of_two(n) else (i + o) % n


def gather_offsets(rb, ca):
    half = ca // 2
    even = [(o, 0) for o in range(1, rb)] + [(0, o) for o in range(1, half)]
    odd = [(0, o) for o in range(half, ca)]
    return [(even[k % len(even)], odd[k % len(odd)]) for k in range(max(len(even), len(odd)))]


def came_from(i, o, n):
    if is_power_of_two(n):
        return lax.bitwise_xor(i, jnp.int32(o)) if not isinstance(o, jax.Array) else lax.bitwise_xor(i, o)
    return lax.rem(i - o + n, n)


def parts_of(v):
    a = v.astype(BF16).astype(F32)
    r = v - a
    b = r.astype(BF16).astype(F32)
    return a, b, r - b


def root_of(x):
    v = jnp.sqrt(x)
    high = v.astype(BF16).astype(F32)
    low = v - high
    left = ((x - high * high) - 2.0 * high * low) - low * low
    return jnp.where(x > 0.0, v + left * (0.5 / v), 0.0)


def key_of(core):
    square = core * core
    whole = jnp.floor(square + 0.5)
    return jnp.where(root_of(whole) == core, whole, square)


def flat_index(cols):
    return lax.axis_index("row") * cols + lax.axis_index("col")


def pack_kernel(p_hbm, label_hbm, core_hbm, out_ref, x_ref, label_ref, core_ref, sems):
    copies = [
        pltpu.make_async_copy(source, target, sems.at[k])
        for k, (source, target) in enumerate(((p_hbm, x_ref), (label_hbm, label_ref), (core_hbm, core_ref)))
    ]
    for copy in copies:
        copy.start()
    for copy in copies:
        copy.wait()
    x = x_ref[...]
    out_ref[0:LANES, :] = x
    xf = x.astype(F32)
    square = xf * xf
    high = square.astype(BF16)
    low = (square - high.astype(F32)).astype(BF16)
    ones = jnp.ones((META, LANES), BF16)
    norm = lax.dot_general(ones, high, NT, preferred_element_type=F32)
    norm = norm + lax.dot_general(ones, low, NT, preferred_element_type=F32)
    core = jnp.broadcast_to(core_ref[...], (META, LANES))
    label = jnp.broadcast_to(label_ref[...].astype(F32), (META, LANES))
    row = lax.broadcasted_iota(jnp.int32, (META, LANES), 0)
    meta = jnp.zeros((META, LANES), F32)
    for k, part in enumerate((*parts_of(norm), *parts_of(core), label)):
        meta = jnp.where(row == k, part, meta)
    both = jnp.concatenate([meta, jnp.zeros((META, LANES), F32)], axis=0)
    out_ref[LANES:, :] = both.astype(BF16)


def join_kernel(cols, own_ref, other_ref, out_ref):
    core = lax.rem(flat_index(cols), 2)
    out_ref[pl.ds(pl.multiple_of(core * LANES, LANES), LANES), :] = own_ref[0:LANES, :]
    out_ref[pl.ds(pl.multiple_of((1 - core) * LANES, LANES), LANES), :] = other_ref[0:LANES, :]
    own = own_ref[LANES:, :].astype(F32)[0:META]
    other = other_ref[LANES:, :].astype(F32)[0:META]
    even = jnp.concatenate([own, other], axis=0)
    odd = jnp.concatenate([other, own], axis=0)
    out_ref[2 * LANES :, :] = jnp.where(core == 0, even, odd).astype(BF16)


def core_of(m8):
    row = lax.broadcasted_iota(jnp.int32, (META, LANES), 0)
    return jnp.sum(jnp.where((row >= 3) & (row < 6), m8, 0.0), axis=0, keepdims=True)


def features(m8, left):
    row = lax.broadcasted_iota(jnp.int32, (2 * META, LANES), 0)
    label = jnp.broadcast_to(m8[6:7], row.shape).astype(jnp.int32)
    same = jnp.where(row == label, 1.0 if left else SAME, 0.0)
    padded = jnp.concatenate([m8, jnp.zeros((META, LANES), F32)], axis=0)
    if left:
        rest = jnp.where(row < 3, padded, jnp.where(row < 6, 1.0, 0.0))
    else:
        rest = jnp.where(row < 3, 1.0, jnp.where(row < 6, pltpu.roll(padded, 3, 0), 0.0))
    return jnp.concatenate([same, rest], axis=0).astype(BF16)


def put_rows(k, ref, which, xr, fr, core_i):
    x = ref[pl.ds(pl.multiple_of(which * LANES, LANES), LANES), :]
    xr[k * LANES : (k + 1) * LANES, :] = (x.astype(F32) * -2.0).astype(BF16)
    meta = ref[2 * LANES :, :].astype(F32)
    m8 = jnp.where(which == 0, meta[0:META], meta[META:])
    fr[:, k * LANES : (k + 1) * LANES] = features(m8, False)
    core_i[0:1, k * LANES : (k + 1) * LANES] = core_of(m8)


def nearest(outs, segments, xr, fr, core_i, t_ref, source_of):
    width = 2 * LANES
    blocks, groups_of = len(outs), (width // 8, 8, LANES)

    def over(segments, body, start):
        base = 0
        for xl, fl, key_ref, offsets in segments:
            step = functools.partial(body, base, xl, fl, key_ref, offsets)
            start = lax.fori_loop(0, len(offsets), step, start, unroll=len(offsets) <= 8)
            base += len(offsets)
        return start

    def first_pass(base, xl, fl, key_ref, offsets, k, best):
        at = pl.multiple_of(k * width, width)
        s = lax.dot_general(xl[pl.ds(at, width), :], xr[...], NT, preferred_element_type=F32)
        s = s + lax.dot_general(fl[:, pl.ds(at, width)], fr[...], TN, preferred_element_type=F32)
        key = key_ref[pl.ds(at, width), :]
        out = []
        for r in range(blocks):
            t = jnp.maximum(s[:, r * LANES : (r + 1) * LANES], key)
            t_ref[pl.ds(at + base * width, width), r * LANES : (r + 1) * LANES] = t
            out.append(jnp.minimum(best[r], jnp.min(t.reshape(groups_of), axis=0)))
        return tuple(out)

    start = tuple(jnp.full((8, LANES), jnp.inf, F32) for _ in outs)
    best = over(segments, first_pass, start)

    values, limits = [], []
    for r in range(blocks):
        least = jnp.min(best[r], axis=0, keepdims=True)
        mine = core_i[0:1, r * LANES : (r + 1) * LANES]
        none = least > FAR
        root = root_of(least)
        values.append(jnp.where(none, jnp.inf, jnp.maximum(mine, root)))
        base = jnp.maximum(least, key_of(mine))
        limit = jnp.where(root_of(least + 1.0) == root, least + 1.0, least)
        limit = jnp.where(root_of(least + 2.0) == root, least + 2.0, limit)
        limits.append(jnp.where(none, jnp.inf, jnp.where(least > 2.0**21, limit, base)))

    step = lax.broadcasted_iota(jnp.int32, groups_of, 0) * 8
    step = (step + lax.broadcasted_iota(jnp.int32, groups_of, 1)).astype(F32)

    def second_pass(base, xl, fl, key_ref, offsets, k, place):
        at = pl.multiple_of((base + k) * width, width)
        offset = sum(jnp.where(k == i, o, 0) for i, o in enumerate(offsets))
        here = step + (source_of(offset) * width).astype(F32)
        out = []
        for r in range(blocks):
            t = t_ref[pl.ds(at, width), r * LANES : (r + 1) * LANES].reshape(groups_of)
            found = jnp.where(t <= limits[r][None], here, jnp.inf)
            out.append(jnp.minimum(place[r], jnp.min(found, axis=0)))
        return tuple(out)

    place = over(segments, second_pass, start)
    for r in range(blocks):
        outs[r][0:1, :] = values[r]
        outs[r][1:2, :] = jnp.min(place[r], axis=0, keepdims=True)


def position(cols, ca):
    me = flat_index(cols)
    chip = lax.div(me, 2)
    return lax.rem(me, 2), lax.div(chip, ca), lax.rem(chip, ca)


def split_of(rb, ca):
    steps = gather_offsets(rb, ca)
    early = [k for k in range((len(steps) + 1) // 2, len(steps)) if not any(o[0] for o in steps[k])]
    late = [k for k in range(len(steps)) if k not in early]
    first = [0, *dict.fromkeys(o[1] for k in early for o in steps[k])]
    second = [*dict.fromkeys(o[1] for k in late for o in steps[k] if not o[0] and o[1] not in first)]
    return early, late, first, second


def put_columns(slot, ref, xl, fl, ck):
    row16 = lax.broadcasted_iota(jnp.int32, (2 * META, LANES), 0)
    xl[slot * 2 * LANES : (slot + 1) * 2 * LANES, :] = ref[0 : 2 * LANES, :]
    meta = ref[2 * LANES :, :].astype(F32)
    for h in range(2):
        m8 = meta[h * META : (h + 1) * META]
        at = (2 * slot + h) * LANES
        fl[:, at : at + LANES] = features(m8, True)
        key = jnp.broadcast_to(key_of(core_of(m8)), (2 * META, LANES))
        p0, p1, p2 = parts_of(key)
        ck[:, at : at + LANES] = jnp.where(
            row16 == 0, p0, jnp.where(row16 == 1, p1, jnp.where(row16 == 2, p2, 0.0))
        ).astype(BF16)


def put_gathered(rb, ca, which, core, got, swapped, offsets, columns, rows=None):
    steps = gather_offsets(rb, ca)

    def put_all(mine):
        seen = set()
        for k, first, second in zip(which, got, swapped):
            for side in range(2):
                offset = steps[k][side]
                if offset in seen:
                    continue
                seen.add(offset)
                ref = first if side == mine else second
                if offset[0]:
                    put_rows(offset[0] - 1, ref, 1 - core, *rows)
                elif offset[1] in offsets:
                    put_columns(offsets.index(offset[1]), ref, *columns)

    for side in range(2):
        pl.when(core == side)(functools.partial(put_all, side))


def spread(ck, key_ref):
    take = jnp.where(lax.broadcasted_iota(jnp.int32, (2 * META, LANES), 0) < 3, 1.0, 0.0).astype(BF16)
    key_ref[...] = lax.dot_general(ck[...], take, TN, preferred_element_type=F32)


def early_kernel(cols, rb, ca, own_ref, *refs):
    early, _, offsets, _ = split_of(rb, ca)
    n = len(early)
    got, swapped, (xl, fl, key_ref, ck) = refs[:n], refs[n : 2 * n], refs[2 * n :]
    core = lax.rem(flat_index(cols), 2)
    put_columns(0, own_ref, xl, fl, ck)
    put_gathered(rb, ca, early, core, got, swapped, offsets, (xl, fl, ck))
    spread(ck, key_ref)


def far_kernel(cols, rb, ca, *refs):
    _, late, first, second = split_of(rb, ca)
    n = len(late)
    ready, refs = refs[:3], refs[3:]
    got, swapped = refs[:n], refs[n : 2 * n]
    xl, fl, key_ref, *outs = refs[2 * n : 3 + 2 * n + rb - 1]
    xr, fr, ck, core_i, t_ref = refs[3 + 2 * n + rb - 1 :]
    core, a, b = position(cols, ca)
    put_gathered(rb, ca, late, core, got, swapped, second, (xl, fl, ck), (xr, fr, core_i))
    spread(ck, key_ref)
    segments = [(*ready, first), (xl, fl, key_ref, second)]
    nearest(outs, segments, xr, fr, core_i, t_ref, lambda o: a * ca + came_from(b, o, ca))


def near_kernel(cols, rb, ca, own_ref, *refs):
    _, _, first, second = split_of(rb, ca)
    out_ref, xr, fr, core_i, t_ref = refs[6:]
    core, a, b = position(cols, ca)
    put_rows(0, own_ref, core, xr, fr, core_i)
    segments = [(*refs[:3], first), (*refs[3:6], second)]
    nearest([out_ref], segments, xr, fr, core_i, t_ref, lambda o: a * ca + came_from(b, o, ca))


def merge_kernel(*refs):
    ins, (value_ref, place_ref) = refs[:-2], refs[-2:]
    value, place = ins[0][0:1, :], ins[0][1:2, :]
    for ref in ins[1:]:
        v, p = ref[0:1, :], ref[1:2, :]
        take = (v < value) | ((v == value) & (p < place))
        value, place = jnp.where(take, v, value), jnp.where(take, p, place)
    value_ref[...] = value
    place_ref[...] = place.astype(jnp.int32)


def shards(rows, cols, points, labels, core):
    count = points.shape[0]
    devices = rows * cols
    chips = devices // 2
    rb = 1
    while rb * rb * 8 <= chips:
        rb *= 2
    ca = chips // rb
    axes = ("row", "col")
    vmem = pl.BlockSpec(memory_space=pltpu.VMEM)

    def call(kernel, shapes, *args, scratch=(), grant=4 << 20, space=pltpu.VMEM):
        single = not isinstance(shapes, (tuple, list))
        return pl.pallas_call(
            kernel,
            out_shape=shapes,
            in_specs=[pl.BlockSpec(memory_space=space)] * len(args),
            out_specs=vmem if single else [vmem] * len(shapes),
            scratch_shapes=list(scratch),
            compiler_params=pltpu.CompilerParams(vmem_limit_bytes=grant),
        )(*args)

    def swap(x):
        return lax.ppermute(x, axes, [(d, d ^ 1) for d in range(devices)])

    def chip_to(chip, offset):
        a, b = divmod(chip, ca)
        return moved(a, offset[0], rb) * ca + moved(b, offset[1], ca)

    inputs = (points, labels.reshape(1, count), core.reshape(1, count))
    own = call(
        pack_kernel,
        jax.ShapeDtypeStruct((count + 2 * META, LANES), BF16),
        *(pltpu.with_memory_space_constraint(x, pltpu.HBM) for x in inputs),
        space=pltpu.HBM,
        scratch=[pltpu.VMEM(x.shape, x.dtype) for x in inputs] + [pltpu.SemaphoreType.DMA((len(inputs),))],
    )
    block = call(
        functools.partial(join_kernel, cols),
        jax.ShapeDtypeStruct((2 * count + 2 * META, LANES), BF16),
        own,
        swap(own),
    )

    got = []
    for offsets in gather_offsets(rb, ca):
        pairs = [(2 * q + side, 2 * chip_to(q, offsets[side]) + side) for q in range(chips) for side in range(2)]
        got.append(lax.ppermute(block, axes, pairs))
    swapped = [swap(x) for x in got]

    wide, far = 2 * count * ca, count * (rb - 1)
    early, late, first_offsets, second_offsets = split_of(rb, ca)

    def held(offsets):
        n = 2 * count * len(offsets)
        shapes = (((n, LANES), BF16), ((32, n), BF16), ((n, LANES), F32))
        return [jax.ShapeDtypeStruct(*x) for x in shapes], pltpu.VMEM((2 * META, n), BF16)

    def row_scratch(n):
        return [pltpu.VMEM((n, LANES), BF16), pltpu.VMEM((32, n), BF16)], [pltpu.VMEM((8, n), F32), pltpu.VMEM((wide, n), F32)]

    shapes, ck = held(first_offsets)
    ready = call(
        functools.partial(early_kernel, cols, rb, ca),
        shapes,
        block,
        *(got[k] for k in early),
        *(swapped[k] for k in early),
        scratch=[ck],
    )
    found = jax.ShapeDtypeStruct((8, LANES), F32)
    shapes, ck = held(second_offsets)
    first, last = row_scratch(far)
    results = call(
        functools.partial(far_kernel, cols, rb, ca),
        [*shapes, *[found] * (rb - 1)],
        *ready,
        *(got[k] for k in late),
        *(swapped[k] for k in late),
        scratch=[*first, ck, *last],
        grant=(6 << 20) + 2 * wide * far * 4,
    )
    columns, partial = [*ready, *results[:3]], results[3:]
    back = []
    for k in range(1, rb):
        pairs = [(d, 2 * chip_to(d // 2, (k, 0)) + 1 - d % 2) for d in range(devices)]
        back.append(lax.ppermute(partial[k - 1], axes, pairs))
    first, last = row_scratch(count)
    own_found = call(
        functools.partial(near_kernel, cols, rb, ca),
        found,
        block,
        *columns,
        scratch=[*first, *last],
        grant=(6 << 20) + 2 * wide * count * 4,
    )
    back.insert(0, own_found)
    value, place = call(
        merge_kernel,
        [jax.ShapeDtypeStruct((1, count), F32), jax.ShapeDtypeStruct((1, count), jnp.int32)],
        *back,
    )
    return value.reshape(count), place.reshape(count)


def solution(mesh):
    rows, cols = mesh.shape["row"], mesh.shape["col"]
    return jax.shard_map(
        functools.partial(shards, rows, cols),
        mesh=mesh,
        in_specs=(P(("row", "col"), None), P(("row", "col")), P(("row", "col"))),
        out_specs=(P(("row", "col")), P(("row", "col"))),
        check_vma=False,
    )
```

```python
import functools

import jax
import jax.numpy as jnp
from jax import lax
from jax.experimental import pallas as pl
from jax.experimental.pallas import tpu as pltpu
from jax.sharding import PartitionSpec as P


META = 8
SAME = 2.0**30
FAR = 2.0**28
LANES = 128
F32 = jnp.float32
BF16 = jnp.bfloat16
NT = (((1,), (1,)), ((), ()))
TN = (((0,), (0,)), ((), ()))


def is_power_of_two(n):
    return n & (n - 1) == 0


def moved(i, o, n):
    return i ^ o if is_power_of_two(n) else (i + o) % n


def gather_offsets(rb, ca):
    half = ca // 2
    even = [(o, 0) for o in range(1, rb)] + [(0, o) for o in range(1, half)]
    odd = [(0, o) for o in range(half, ca)]
    return [(even[k % len(even)], odd[k % len(odd)]) for k in range(max(len(even), len(odd)))]


def came_from(i, o, n):
    if is_power_of_two(n):
        return lax.bitwise_xor(i, jnp.int32(o)) if not isinstance(o, jax.Array) else lax.bitwise_xor(i, o)
    return lax.rem(i - o + n, n)


def parts_of(v):
    a = v.astype(BF16).astype(F32)
    r = v - a
    b = r.astype(BF16).astype(F32)
    return a, b, r - b


def root_of(x):
    v = jnp.sqrt(x)
    high = v.astype(BF16).astype(F32)
    low = v - high
    left = ((x - high * high) - 2.0 * high * low) - low * low
    return jnp.where(x > 0.0, v + left * (0.5 / v), 0.0)


def key_of(core):
    square = core * core
    whole = jnp.floor(square + 0.5)
    return jnp.where(root_of(whole) == core, whole, square)


def flat_index(cols):
    return lax.axis_index("row") * cols + lax.axis_index("col")


def pack_kernel(p_hbm, label_hbm, core_hbm, out_ref, x_ref, label_ref, core_ref, sems):
    copies = [
        pltpu.make_async_copy(source, target, sems.at[k])
        for k, (source, target) in enumerate(((p_hbm, x_ref), (label_hbm, label_ref), (core_hbm, core_ref)))
    ]
    for copy in copies:
        copy.start()
    for copy in copies:
        copy.wait()
    x = x_ref[...]
    out_ref[0:LANES, :] = x
    xf = x.astype(F32)
    square = xf * xf
    high = square.astype(BF16)
    low = (square - high.astype(F32)).astype(BF16)
    ones = jnp.ones((META, LANES), BF16)
    norm = lax.dot_general(ones, high, NT, preferred_element_type=F32)
    norm = norm + lax.dot_general(ones, low, NT, preferred_element_type=F32)
    core = jnp.broadcast_to(core_ref[...], (META, LANES))
    label = jnp.broadcast_to(label_ref[...].astype(F32), (META, LANES))
    row = lax.broadcasted_iota(jnp.int32, (META, LANES), 0)
    meta = jnp.zeros((META, LANES), F32)
    for k, part in enumerate((*parts_of(norm), *parts_of(core), label)):
        meta = jnp.where(row == k, part, meta)
    both = jnp.concatenate([meta, jnp.zeros((META, LANES), F32)], axis=0)
    out_ref[LANES:, :] = both.astype(BF16)


def join_kernel(cols, own_ref, other_ref, out_ref):
    core = lax.rem(flat_index(cols), 2)
    out_ref[pl.ds(pl.multiple_of(core * LANES, LANES), LANES), :] = own_ref[0:LANES, :]
    out_ref[pl.ds(pl.multiple_of((1 - core) * LANES, LANES), LANES), :] = other_ref[0:LANES, :]
    own = own_ref[LANES:, :].astype(F32)[0:META]
    other = other_ref[LANES:, :].astype(F32)[0:META]
    even = jnp.concatenate([own, other], axis=0)
    odd = jnp.concatenate([other, own], axis=0)
    out_ref[2 * LANES :, :] = jnp.where(core == 0, even, odd).astype(BF16)


def core_of(m8):
    row = lax.broadcasted_iota(jnp.int32, (META, LANES), 0)
    return jnp.sum(jnp.where((row >= 3) & (row < 6), m8, 0.0), axis=0, keepdims=True)


def features(m8, left):
    row = lax.broadcasted_iota(jnp.int32, (2 * META, LANES), 0)
    label = jnp.broadcast_to(m8[6:7], row.shape).astype(jnp.int32)
    same = jnp.where(row == label, 1.0 if left else SAME, 0.0)
    padded = jnp.concatenate([m8, jnp.zeros((META, LANES), F32)], axis=0)
    if left:
        rest = jnp.where(row < 3, padded, jnp.where(row < 6, 1.0, 0.0))
    else:
        rest = jnp.where(row < 3, 1.0, jnp.where(row < 6, pltpu.roll(padded, 3, 0), 0.0))
    return jnp.concatenate([same, rest], axis=0).astype(BF16)


def put_rows(k, ref, which, xr, fr, core_i):
    x = jnp.where(which == 0, ref[0:LANES, :], ref[LANES : 2 * LANES, :])
    xr[k * LANES : (k + 1) * LANES, :] = (x.astype(F32) * -2.0).astype(BF16)
    meta = ref[2 * LANES :, :].astype(F32)
    m8 = jnp.where(which == 0, meta[0:META], meta[META:])
    fr[:, k * LANES : (k + 1) * LANES] = features(m8, False)
    core_i[0:1, k * LANES : (k + 1) * LANES] = core_of(m8)


def nearest(outs, segments, xr, fr, core_i, t_ref, source_of):
    width = 2 * LANES
    blocks, groups_of = len(outs), (width // 8, 8, LANES)

    def over(segments, body, start):
        base = 0
        for xl, fl, key_ref, offsets in segments:
            if body is first_pass and len(offsets) <= 8:
                s = product(xl[...], fl[...])
                for k in range(len(offsets)):
                    start = body(base, xl, fl, key_ref, offsets, k, start, s[k * width : (k + 1) * width])
                base += len(offsets)
                continue
            step = functools.partial(body, base, xl, fl, key_ref, offsets)
            start = lax.fori_loop(0, len(offsets), step, start, unroll=len(offsets) <= 8)
            base += len(offsets)
        return start

    def product(x, f):
        s = lax.dot_general(x, xr[...], NT, preferred_element_type=F32)
        return s + lax.dot_general(f, fr[...], TN, preferred_element_type=F32)

    def first_pass(base, xl, fl, key_ref, offsets, k, best, s=None):
        at = k * width if s is not None else pl.multiple_of(k * width, width)
        if s is None:
            s = product(xl[pl.ds(at, width), :], fl[:, pl.ds(at, width)])
        key = key_ref[pl.ds(at, width), :]
        out = []
        for r in range(blocks):
            t = jnp.maximum(s[:, r * LANES : (r + 1) * LANES], key)
            t_ref[pl.ds(at + base * width, width), r * LANES : (r + 1) * LANES] = t
            out.append(jnp.minimum(best[r], jnp.min(t.reshape(groups_of), axis=0)))
        return tuple(out)

    start = tuple(jnp.full((8, LANES), jnp.inf, F32) for _ in outs)
    best = over(segments, first_pass, start)

    values, limits = [], []
    for r in range(blocks):
        least = jnp.min(best[r], axis=0, keepdims=True)
        mine = core_i[0:1, r * LANES : (r + 1) * LANES]
        none = least > FAR
        root = root_of(least)
        values.append(jnp.where(none, jnp.inf, jnp.maximum(mine, root)))
        base = jnp.maximum(least, key_of(mine))
        limit = jnp.where(root_of(least + 1.0) == root, least + 1.0, least)
        limit = jnp.where(root_of(least + 2.0) == root, least + 2.0, limit)
        limits.append(jnp.where(none, jnp.inf, jnp.where(least > 2.0**21, limit, base)))

    within = lax.broadcasted_iota(jnp.int32, (8, LANES), 0).astype(F32)

    def second_pass(base, xl, fl, key_ref, offsets, k, place):
        at = pl.multiple_of((base + k) * width, width)
        offset = sum(jnp.where(k == i, o, 0) for i, o in enumerate(offsets))
        here = within + (source_of(offset) * width).astype(F32)
        out = []
        for r in range(blocks):
            t = t_ref[pl.ds(at, width), r * LANES : (r + 1) * LANES].reshape(groups_of)
            found = jnp.full((8, LANES), jnp.inf, F32)
            for g in range(width // 8 - 1, -1, -1):
                found = jnp.where(t[g] <= limits[r], 8.0 * g, found)
            out.append(jnp.minimum(place[r], found + here))
        return tuple(out)

    place = over(segments, second_pass, start)
    for r in range(blocks):
        outs[r][0:1, :] = values[r]
        outs[r][1:2, :] = jnp.min(place[r], axis=0, keepdims=True)


def position(cols, ca):
    me = flat_index(cols)
    chip = lax.div(me, 2)
    return lax.rem(me, 2), lax.div(chip, ca), lax.rem(chip, ca)


def split_of(rb, ca):
    steps = gather_offsets(rb, ca)
    early = [k for k in range((len(steps) + 1) // 2, len(steps)) if not any(o[0] for o in steps[k])]
    late = [k for k in range(len(steps)) if k not in early]
    first = [0, *dict.fromkeys(o[1] for k in early for o in steps[k])]
    second = [*dict.fromkeys(o[1] for k in late for o in steps[k] if not o[0] and o[1] not in first)]
    return early, late, first, second


def put_columns(slot, ref, xl, fl, ck):
    row16 = lax.broadcasted_iota(jnp.int32, (2 * META, LANES), 0)
    xl[slot * 2 * LANES : (slot + 1) * 2 * LANES, :] = ref[0 : 2 * LANES, :]
    meta = ref[2 * LANES :, :].astype(F32)
    for h in range(2):
        m8 = meta[h * META : (h + 1) * META]
        at = (2 * slot + h) * LANES
        fl[:, at : at + LANES] = features(m8, True)
        key = jnp.broadcast_to(key_of(core_of(m8)), (2 * META, LANES))
        p0, p1, p2 = parts_of(key)
        ck[:, at : at + LANES] = jnp.where(
            row16 == 0, p0, jnp.where(row16 == 1, p1, jnp.where(row16 == 2, p2, 0.0))
        ).astype(BF16)


def put_gathered(rb, ca, which, core, got, swapped, offsets, columns, rows=None):
    steps = gather_offsets(rb, ca)
    seen = set()
    for k, first, second in zip(which, got, swapped):
        for side in range(2):
            offset = steps[k][side]
            if offset in seen:
                continue
            seen.add(offset)
            block = jnp.where(core == side, first[...], second[...])
            if offset[0]:
                put_rows(offset[0] - 1, block, 1 - core, *rows)
            elif offset[1] in offsets:
                put_columns(offsets.index(offset[1]), block, *columns)


def spread(ck, key_ref):
    take = jnp.where(lax.broadcasted_iota(jnp.int32, (2 * META, LANES), 0) < 3, 1.0, 0.0).astype(BF16)
    key_ref[...] = lax.dot_general(ck[...], take, TN, preferred_element_type=F32)


def early_kernel(cols, rb, ca, own_ref, *refs):
    early, _, offsets, _ = split_of(rb, ca)
    n = len(early)
    got, swapped, (xl, fl, key_ref, ck) = refs[:n], refs[n : 2 * n], refs[2 * n :]
    core = lax.rem(flat_index(cols), 2)
    put_columns(0, own_ref, xl, fl, ck)
    put_gathered(rb, ca, early, core, got, swapped, offsets, (xl, fl, ck))
    spread(ck, key_ref)


def far_kernel(cols, rb, ca, *refs):
    _, late, first, second = split_of(rb, ca)
    n = len(late)
    ready, refs = refs[:3], refs[3:]
    got, swapped = refs[:n], refs[n : 2 * n]
    xl, fl, key_ref, *outs = refs[2 * n : 3 + 2 * n + rb - 1]
    xr, fr, ck, core_i, t_ref = refs[3 + 2 * n + rb - 1 :]
    core, a, b = position(cols, ca)
    put_gathered(rb, ca, late, core, got, swapped, second, (xl, fl, ck), (xr, fr, core_i))
    spread(ck, key_ref)
    segments = [(*ready, first), (xl, fl, key_ref, second)]
    nearest(outs, segments, xr, fr, core_i, t_ref, lambda o: a * ca + came_from(b, o, ca))


def near_kernel(cols, rb, ca, own_ref, *refs):
    _, _, first, second = split_of(rb, ca)
    out_ref, xr, fr, core_i, t_ref = refs[6:]
    core, a, b = position(cols, ca)
    put_rows(0, own_ref, core, xr, fr, core_i)
    segments = [(*refs[:3], first), (*refs[3:6], second)]
    nearest([out_ref], segments, xr, fr, core_i, t_ref, lambda o: a * ca + came_from(b, o, ca))


def merge_kernel(*refs):
    ins, (value_ref, place_ref) = refs[:-2], refs[-2:]
    value, place = ins[0][0:1, :], ins[0][1:2, :]
    for ref in ins[1:]:
        v, p = ref[0:1, :], ref[1:2, :]
        take = (v < value) | ((v == value) & (p < place))
        value, place = jnp.where(take, v, value), jnp.where(take, p, place)
    value_ref[...] = value
    place_ref[...] = place.astype(jnp.int32)


def shards(rows, cols, points, labels, core):
    count = points.shape[0]
    devices = rows * cols
    chips = devices // 2
    rb = 1
    while rb * rb * 8 <= chips:
        rb *= 2
    ca = chips // rb
    axes = ("row", "col")
    vmem = pl.BlockSpec(memory_space=pltpu.VMEM)

    def call(kernel, shapes, *args, scratch=(), grant=4 << 20, space=pltpu.VMEM):
        single = not isinstance(shapes, (tuple, list))
        return pl.pallas_call(
            kernel,
            out_shape=shapes,
            in_specs=[pl.BlockSpec(memory_space=space)] * len(args),
            out_specs=vmem if single else [vmem] * len(shapes),
            scratch_shapes=list(scratch),
            compiler_params=pltpu.CompilerParams(vmem_limit_bytes=grant),
        )(*args)

    def swap(x):
        return lax.ppermute(x, axes, [(d, d ^ 1) for d in range(devices)])

    def chip_to(chip, offset):
        a, b = divmod(chip, ca)
        return moved(a, offset[0], rb) * ca + moved(b, offset[1], ca)

    inputs = (points, labels.reshape(1, count), core.reshape(1, count))
    own = call(
        pack_kernel,
        jax.ShapeDtypeStruct((count + 2 * META, LANES), BF16),
        *(pltpu.with_memory_space_constraint(x, pltpu.HBM) for x in inputs),
        space=pltpu.HBM,
        scratch=[pltpu.VMEM(x.shape, x.dtype) for x in inputs] + [pltpu.SemaphoreType.DMA((len(inputs),))],
    )
    block = call(
        functools.partial(join_kernel, cols),
        jax.ShapeDtypeStruct((2 * count + 2 * META, LANES), BF16),
        own,
        swap(own),
    )

    got = []
    for offsets in gather_offsets(rb, ca):
        pairs = [(2 * q + side, 2 * chip_to(q, offsets[side]) + side) for q in range(chips) for side in range(2)]
        got.append(lax.ppermute(block, axes, pairs))
    swapped = [swap(x) for x in got]

    wide, far = 2 * count * ca, count * (rb - 1)
    early, late, first_offsets, second_offsets = split_of(rb, ca)

    def held(offsets):
        n = 2 * count * len(offsets)
        shapes = (((n, LANES), BF16), ((32, n), BF16), ((n, LANES), F32))
        return [jax.ShapeDtypeStruct(*x) for x in shapes], pltpu.VMEM((2 * META, n), BF16)

    def row_scratch(n):
        return [pltpu.VMEM((n, LANES), BF16), pltpu.VMEM((32, n), BF16)], [pltpu.VMEM((8, n), F32), pltpu.VMEM((wide, n), F32)]

    shapes, ck = held(first_offsets)
    ready = call(
        functools.partial(early_kernel, cols, rb, ca),
        shapes,
        block,
        *(got[k] for k in early),
        *(swapped[k] for k in early),
        scratch=[ck],
    )
    found = jax.ShapeDtypeStruct((8, LANES), F32)
    shapes, ck = held(second_offsets)
    first, last = row_scratch(far)
    results = call(
        functools.partial(far_kernel, cols, rb, ca),
        [*shapes, *[found] * (rb - 1)],
        *ready,
        *(got[k] for k in late),
        *(swapped[k] for k in late),
        scratch=[*first, ck, *last],
        grant=(6 << 20) + 2 * wide * far * 4,
    )
    columns, partial = [*ready, *results[:3]], results[3:]
    back = []
    for k in range(1, rb):
        pairs = [(d, 2 * chip_to(d // 2, (k, 0)) + 1 - d % 2) for d in range(devices)]
        back.append(lax.ppermute(partial[k - 1], axes, pairs))
    first, last = row_scratch(count)
    own_found = call(
        functools.partial(near_kernel, cols, rb, ca),
        found,
        block,
        *columns,
        scratch=[*first, *last],
        grant=(6 << 20) + 2 * wide * count * 4,
    )
    back.insert(0, own_found)
    value, place = call(
        merge_kernel,
        [jax.ShapeDtypeStruct((1, count), F32), jax.ShapeDtypeStruct((1, count), jnp.int32)],
        *back,
    )
    return value.reshape(count), place.reshape(count)


def solution(mesh):
    rows, cols = mesh.shape["row"], mesh.shape["col"]
    return jax.shard_map(
        functools.partial(shards, rows, cols),
        mesh=mesh,
        in_specs=(P(("row", "col"), None), P(("row", "col")), P(("row", "col"))),
        out_specs=(P(("row", "col")), P(("row", "col"))),
        check_vma=False,
    )
```

```python
import functools

import jax
import jax.numpy as jnp
from jax import lax
from jax.experimental import pallas as pl
from jax.experimental.pallas import tpu as pltpu
from jax.sharding import PartitionSpec as P


META = 8
SAME = 2.0**30
FAR = 2.0**28
LANES = 128
F32 = jnp.float32
BF16 = jnp.bfloat16
NT = (((1,), (1,)), ((), ()))
TN = (((0,), (0,)), ((), ()))


def is_power_of_two(n):
    return n & (n - 1) == 0


def moved(i, o, n):
    return i ^ o if is_power_of_two(n) else (i + o) % n


def gather_offsets(rb, ca):
    half = ca // 2
    even = [(o, 0) for o in range(1, rb)] + [(0, o) for o in range(1, half)]
    odd = [(0, o) for o in range(half, ca)]
    return [(even[k % len(even)], odd[k % len(odd)]) for k in range(max(len(even), len(odd)))]


def came_from(i, o, n):
    if is_power_of_two(n):
        return lax.bitwise_xor(i, jnp.int32(o)) if not isinstance(o, jax.Array) else lax.bitwise_xor(i, o)
    return lax.rem(i - o + n, n)


def parts_of(v):
    a = v.astype(BF16).astype(F32)
    r = v - a
    b = r.astype(BF16).astype(F32)
    return a, b, r - b


def root_of(x):
    v = jnp.sqrt(x)
    high = v.astype(BF16).astype(F32)
    low = v - high
    left = ((x - high * high) - 2.0 * high * low) - low * low
    return jnp.where(x > 0.0, v + left * (0.5 / v), 0.0)


def key_of(core):
    square = core * core
    whole = jnp.floor(square + 0.5)
    return jnp.where(root_of(whole) == core, whole, square)


def flat_index(cols):
    return lax.axis_index("row") * cols + lax.axis_index("col")


def pack_kernel(p_hbm, label_hbm, core_hbm, out_ref, label_ref, core_ref, sems):
    targets = ((p_hbm, out_ref.at[0:LANES, :]), (label_hbm, label_ref), (core_hbm, core_ref))
    copies = [pltpu.make_async_copy(source, target, sems.at[k]) for k, (source, target) in enumerate(targets)]
    for copy in copies:
        copy.start()
    for copy in copies[1:]:
        copy.wait()
    row = lax.broadcasted_iota(jnp.int32, (META, LANES), 0)
    meta = jnp.where(row == 6, label_ref[...].astype(F32), 0.0)
    for k, part in enumerate(parts_of(jnp.broadcast_to(core_ref[...], (META, LANES)))):
        meta = jnp.where(row == 3 + k, part, meta)
    copies[0].wait()
    xf = out_ref[0:LANES, :].astype(F32)
    square = xf * xf
    high = square.astype(BF16)
    low = (square - high.astype(F32)).astype(BF16)
    ones = jnp.ones((META, LANES), BF16)
    norm = lax.dot_general(ones, high, NT, preferred_element_type=F32)
    norm = norm + lax.dot_general(ones, low, NT, preferred_element_type=F32)
    for k, part in enumerate(parts_of(norm)):
        meta = jnp.where(row == k, part, meta)
    both = jnp.concatenate([meta, jnp.zeros((META, LANES), F32)], axis=0)
    out_ref[LANES:, :] = both.astype(BF16)


def join_kernel(cols, own_ref, other_ref, out_ref):
    core = lax.rem(flat_index(cols), 2)
    out_ref[pl.ds(pl.multiple_of(core * LANES, LANES), LANES), :] = own_ref[0:LANES, :]
    out_ref[pl.ds(pl.multiple_of((1 - core) * LANES, LANES), LANES), :] = other_ref[0:LANES, :]
    own = own_ref[LANES:, :].astype(F32)[0:META]
    other = other_ref[LANES:, :].astype(F32)[0:META]
    even = jnp.concatenate([own, other], axis=0)
    odd = jnp.concatenate([other, own], axis=0)
    out_ref[2 * LANES :, :] = jnp.where(core == 0, even, odd).astype(BF16)


def core_of(m8):
    row = lax.broadcasted_iota(jnp.int32, (META, LANES), 0)
    return jnp.sum(jnp.where((row >= 3) & (row < 6), m8, 0.0), axis=0, keepdims=True)


def features(m8, left):
    row = lax.broadcasted_iota(jnp.int32, (2 * META, LANES), 0)
    label = jnp.broadcast_to(m8[6:7], row.shape).astype(jnp.int32)
    same = jnp.where(row == label, 1.0 if left else SAME, 0.0)
    padded = jnp.concatenate([m8, jnp.zeros((META, LANES), F32)], axis=0)
    if left:
        rest = jnp.where(row < 3, padded, jnp.where(row < 6, 1.0, 0.0))
    else:
        rest = jnp.where(row < 3, 1.0, jnp.where(row < 6, pltpu.roll(padded, 3, 0), 0.0))
    return jnp.concatenate([same, rest], axis=0).astype(BF16)


def put_rows(k, ref, which, xr, fr, core_i):
    x = jnp.where(which == 0, ref[0:LANES, :], ref[LANES : 2 * LANES, :])
    xr[k * LANES : (k + 1) * LANES, :] = (x.astype(F32) * -2.0).astype(BF16)
    meta = ref[2 * LANES :, :].astype(F32)
    m8 = jnp.where(which == 0, meta[0:META], meta[META:])
    fr[:, k * LANES : (k + 1) * LANES] = features(m8, False)
    core_i[0:1, k * LANES : (k + 1) * LANES] = core_of(m8)


def nearest(outs, segments, xr, fr, core_i, t_ref, source_of):
    width = 2 * LANES
    blocks, groups_of = len(outs), (width // 8, 8, LANES)

    def over(segments, body, start):
        base = 0
        for xl, fl, key_ref, offsets in segments:
            if body is first_pass and len(offsets) <= 8:
                s = product(xl[...], fl[...])
                for k in range(len(offsets)):
                    start = body(base, xl, fl, key_ref, offsets, k, start, s[k * width : (k + 1) * width])
                base += len(offsets)
                continue
            step = functools.partial(body, base, xl, fl, key_ref, offsets)
            start = lax.fori_loop(0, len(offsets), step, start, unroll=len(offsets) <= 8)
            base += len(offsets)
        return start

    def product(x, f):
        s = lax.dot_general(x, xr[...], NT, preferred_element_type=F32)
        return s + lax.dot_general(f, fr[...], TN, preferred_element_type=F32)

    def first_pass(base, xl, fl, key_ref, offsets, k, best, s=None):
        at = k * width if s is not None else pl.multiple_of(k * width, width)
        if s is None:
            s = product(xl[pl.ds(at, width), :], fl[:, pl.ds(at, width)])
        key = key_ref[pl.ds(at, width), :]
        out = []
        for r in range(blocks):
            t = jnp.maximum(s[:, r * LANES : (r + 1) * LANES], key)
            t_ref[pl.ds(at + base * width, width), r * LANES : (r + 1) * LANES] = t
            out.append(jnp.minimum(best[r], jnp.min(t.reshape(groups_of), axis=0)))
        return tuple(out)

    start = tuple(jnp.full((8, LANES), jnp.inf, F32) for _ in outs)
    best = over(segments, first_pass, start)

    values, limits = [], []
    for r in range(blocks):
        least = jnp.min(best[r], axis=0, keepdims=True)
        mine = core_i[0:1, r * LANES : (r + 1) * LANES]
        none = least > FAR
        root = root_of(least)
        values.append(jnp.where(none, jnp.inf, jnp.maximum(mine, root)))
        base = jnp.maximum(least, key_of(mine))
        limit = jnp.where(root_of(least + 1.0) == root, least + 1.0, least)
        limit = jnp.where(root_of(least + 2.0) == root, least + 2.0, limit)
        limits.append(jnp.where(none, jnp.inf, jnp.where(least > 2.0**21, limit, base)))

    within = lax.broadcasted_iota(jnp.int32, (8, LANES), 0).astype(F32)

    def second_pass(base, xl, fl, key_ref, offsets, k, place):
        at = pl.multiple_of((base + k) * width, width)
        offset = sum(jnp.where(k == i, o, 0) for i, o in enumerate(offsets))
        here = within + (source_of(offset) * width).astype(F32)
        out = []
        for r in range(blocks):
            t = t_ref[pl.ds(at, width), r * LANES : (r + 1) * LANES].reshape(groups_of)
            found = jnp.full((8, LANES), jnp.inf, F32)
            for g in range(width // 8 - 1, -1, -1):
                found = jnp.where(t[g] <= limits[r], 8.0 * g, found)
            out.append(jnp.minimum(place[r], found + here))
        return tuple(out)

    place = over(segments, second_pass, start)
    for r in range(blocks):
        outs[r][0:1, :] = values[r]
        outs[r][1:2, :] = jnp.min(place[r], axis=0, keepdims=True)


def position(cols, ca):
    me = flat_index(cols)
    chip = lax.div(me, 2)
    return lax.rem(me, 2), lax.div(chip, ca), lax.rem(chip, ca)


def split_of(rb, ca):
    steps = gather_offsets(rb, ca)
    early = [k for k in range((len(steps) + 1) // 2, len(steps)) if not any(o[0] for o in steps[k])]
    late = [k for k in range(len(steps)) if k not in early]
    first = [0, *dict.fromkeys(o[1] for k in early for o in steps[k])]
    second = [*dict.fromkeys(o[1] for k in late for o in steps[k] if not o[0] and o[1] not in first)]
    return early, late, first, second


def put_columns(slot, ref, xl, fl, ck):
    row16 = lax.broadcasted_iota(jnp.int32, (2 * META, LANES), 0)
    xl[slot * 2 * LANES : (slot + 1) * 2 * LANES, :] = ref[0 : 2 * LANES, :]
    meta = ref[2 * LANES :, :].astype(F32)
    for h in range(2):
        m8 = meta[h * META : (h + 1) * META]
        at = (2 * slot + h) * LANES
        fl[:, at : at + LANES] = features(m8, True)
        key = jnp.broadcast_to(key_of(core_of(m8)), (2 * META, LANES))
        p0, p1, p2 = parts_of(key)
        ck[:, at : at + LANES] = jnp.where(
            row16 == 0, p0, jnp.where(row16 == 1, p1, jnp.where(row16 == 2, p2, 0.0))
        ).astype(BF16)


def put_gathered(rb, ca, which, core, got, swapped, offsets, columns, rows=None):
    steps = gather_offsets(rb, ca)
    seen = set()
    for k, first, second in zip(which, got, swapped):
        for side in range(2):
            offset = steps[k][side]
            if offset in seen:
                continue
            seen.add(offset)
            block = jnp.where(core == side, first[...], second[...])
            if offset[0]:
                put_rows(offset[0] - 1, block, 1 - core, *rows)
            elif offset[1] in offsets:
                put_columns(offsets.index(offset[1]), block, *columns)


def spread(ck, key_ref):
    take = jnp.where(lax.broadcasted_iota(jnp.int32, (2 * META, LANES), 0) < 3, 1.0, 0.0).astype(BF16)
    key_ref[...] = lax.dot_general(ck[...], take, TN, preferred_element_type=F32)


def early_kernel(cols, rb, ca, own_ref, *refs):
    early, _, offsets, _ = split_of(rb, ca)
    n = len(early)
    got, swapped, (xl, fl, key_ref, ck) = refs[:n], refs[n : 2 * n], refs[2 * n :]
    core = lax.rem(flat_index(cols), 2)
    put_columns(0, own_ref, xl, fl, ck)
    put_gathered(rb, ca, early, core, got, swapped, offsets, (xl, fl, ck))
    spread(ck, key_ref)


def far_kernel(cols, rb, ca, *refs):
    _, late, first, second = split_of(rb, ca)
    n = len(late)
    ready, refs = refs[:3], refs[3:]
    got, swapped = refs[:n], refs[n : 2 * n]
    xl, fl, key_ref, *outs = refs[2 * n : 3 + 2 * n + rb - 1]
    xr, fr, ck, core_i, t_ref = refs[3 + 2 * n + rb - 1 :]
    core, a, b = position(cols, ca)
    put_gathered(rb, ca, late, core, got, swapped, second, (xl, fl, ck), (xr, fr, core_i))
    spread(ck, key_ref)
    segments = [(*ready, first), (xl, fl, key_ref, second)]
    nearest(outs, segments, xr, fr, core_i, t_ref, lambda o: a * ca + came_from(b, o, ca))


def near_kernel(cols, rb, ca, own_ref, *refs):
    _, _, first, second = split_of(rb, ca)
    out_ref, xr, fr, core_i, t_ref = refs[6:]
    core, a, b = position(cols, ca)
    put_rows(0, own_ref, core, xr, fr, core_i)
    segments = [(*refs[:3], first), (*refs[3:6], second)]
    nearest([out_ref], segments, xr, fr, core_i, t_ref, lambda o: a * ca + came_from(b, o, ca))


def merge_kernel(*refs):
    ins, (value_ref, place_ref) = refs[:-2], refs[-2:]
    value, place = ins[0][0:1, :], ins[0][1:2, :]
    for ref in ins[1:]:
        v, p = ref[0:1, :], ref[1:2, :]
        take = (v < value) | ((v == value) & (p < place))
        value, place = jnp.where(take, v, value), jnp.where(take, p, place)
    value_ref[...] = value
    place_ref[...] = place.astype(jnp.int32)


def shards(rows, cols, points, labels, core):
    count = points.shape[0]
    devices = rows * cols
    chips = devices // 2
    rb = 1
    while rb * rb * 8 <= chips:
        rb *= 2
    ca = chips // rb
    axes = ("row", "col")
    vmem = pl.BlockSpec(memory_space=pltpu.VMEM)

    def call(kernel, shapes, *args, scratch=(), grant=4 << 20, space=pltpu.VMEM):
        single = not isinstance(shapes, (tuple, list))
        return pl.pallas_call(
            kernel,
            out_shape=shapes,
            in_specs=[pl.BlockSpec(memory_space=space)] * len(args),
            out_specs=vmem if single else [vmem] * len(shapes),
            scratch_shapes=list(scratch),
            compiler_params=pltpu.CompilerParams(vmem_limit_bytes=grant),
        )(*args)

    def swap(x):
        return lax.ppermute(x, axes, [(d, d ^ 1) for d in range(devices)])

    def chip_to(chip, offset):
        a, b = divmod(chip, ca)
        return moved(a, offset[0], rb) * ca + moved(b, offset[1], ca)

    inputs = (points, labels.reshape(1, count), core.reshape(1, count))
    own = call(
        pack_kernel,
        jax.ShapeDtypeStruct((count + 2 * META, LANES), BF16),
        *(pltpu.with_memory_space_constraint(x, pltpu.HBM) for x in inputs),
        space=pltpu.HBM,
        scratch=[pltpu.VMEM(x.shape, x.dtype) for x in inputs[1:]] + [pltpu.SemaphoreType.DMA((len(inputs),))],
    )
    block = call(
        functools.partial(join_kernel, cols),
        jax.ShapeDtypeStruct((2 * count + 2 * META, LANES), BF16),
        own,
        swap(own),
    )

    got = []
    for offsets in gather_offsets(rb, ca):
        pairs = [(2 * q + side, 2 * chip_to(q, offsets[side]) + side) for q in range(chips) for side in range(2)]
        got.append(lax.ppermute(block, axes, pairs))
    swapped = [swap(x) for x in got]

    wide, far = 2 * count * ca, count * (rb - 1)
    early, late, first_offsets, second_offsets = split_of(rb, ca)

    def held(offsets):
        n = 2 * count * len(offsets)
        shapes = (((n, LANES), BF16), ((32, n), BF16), ((n, LANES), F32))
        return [jax.ShapeDtypeStruct(*x) for x in shapes], pltpu.VMEM((2 * META, n), BF16)

    def row_scratch(n):
        return [pltpu.VMEM((n, LANES), BF16), pltpu.VMEM((32, n), BF16)], [pltpu.VMEM((8, n), F32), pltpu.VMEM((wide, n), F32)]

    shapes, ck = held(first_offsets)
    ready = call(
        functools.partial(early_kernel, cols, rb, ca),
        shapes,
        block,
        *(got[k] for k in early),
        *(swapped[k] for k in early),
        scratch=[ck],
    )
    found = jax.ShapeDtypeStruct((8, LANES), F32)
    shapes, ck = held(second_offsets)
    first, last = row_scratch(far)
    results = call(
        functools.partial(far_kernel, cols, rb, ca),
        [*shapes, *[found] * (rb - 1)],
        *ready,
        *(got[k] for k in late),
        *(swapped[k] for k in late),
        scratch=[*first, ck, *last],
        grant=(6 << 20) + 2 * wide * far * 4,
    )
    columns, partial = [*ready, *results[:3]], results[3:]
    back = []
    for k in range(1, rb):
        pairs = [(d, 2 * chip_to(d // 2, (k, 0)) + 1 - d % 2) for d in range(devices)]
        back.append(lax.ppermute(partial[k - 1], axes, pairs))
    first, last = row_scratch(count)
    own_found = call(
        functools.partial(near_kernel, cols, rb, ca),
        found,
        block,
        *columns,
        scratch=[*first, *last],
        grant=(6 << 20) + 2 * wide * count * 4,
    )
    back.insert(0, own_found)
    value, place = call(
        merge_kernel,
        [jax.ShapeDtypeStruct((1, count), F32), jax.ShapeDtypeStruct((1, count), jnp.int32)],
        *back,
    )
    return value.reshape(count), place.reshape(count)


def solution(mesh):
    rows, cols = mesh.shape["row"], mesh.shape["col"]
    return jax.shard_map(
        functools.partial(shards, rows, cols),
        mesh=mesh,
        in_specs=(P(("row", "col"), None), P(("row", "col")), P(("row", "col"))),
        out_specs=(P(("row", "col")), P(("row", "col"))),
        check_vma=False,
    )
```

```python
import functools

import jax
import jax.numpy as jnp
from jax import lax
from jax.experimental import pallas as pl
from jax.experimental.pallas import tpu as pltpu
from jax.sharding import PartitionSpec as P


META = 8
SAME = 2.0**30
FAR = 2.0**28
LANES = 128
F32 = jnp.float32
BF16 = jnp.bfloat16
NT = (((1,), (1,)), ((), ()))
TN = (((0,), (0,)), ((), ()))


def is_power_of_two(n):
    return n & (n - 1) == 0


def moved(i, o, n):
    return i ^ o if is_power_of_two(n) else (i + o) % n


def gather_offsets(rb, ca):
    half = ca // 2
    even = [(0, half)] + [(0, o) for o in range(1, half)]
    odd = [(o, 0) for o in range(1, rb)] + [(0, o) for o in range(half + 1, ca)]
    return [(even[k % len(even)], odd[k % len(odd)]) for k in range(max(len(even), len(odd)))]


def came_from(i, o, n):
    if is_power_of_two(n):
        return lax.bitwise_xor(i, jnp.int32(o)) if not isinstance(o, jax.Array) else lax.bitwise_xor(i, o)
    return lax.rem(i - o + n, n)


def parts_of(v):
    a = v.astype(BF16).astype(F32)
    r = v - a
    b = r.astype(BF16).astype(F32)
    return a, b, r - b


def root_of(x):
    v = jnp.sqrt(x)
    high = v.astype(BF16).astype(F32)
    low = v - high
    left = ((x - high * high) - 2.0 * high * low) - low * low
    return jnp.where(x > 0.0, v + left * (0.5 / v), 0.0)


def key_of(core):
    square = core * core
    whole = jnp.floor(square + 0.5)
    return jnp.where(root_of(whole) == core, whole, square)


def flat_index(cols):
    return lax.axis_index("row") * cols + lax.axis_index("col")


def pack_kernel(p_hbm, label_hbm, core_hbm, out_ref, x_ref, label_ref, core_ref, sems):
    copies = [
        pltpu.make_async_copy(source, target, sems.at[k])
        for k, (source, target) in enumerate(((p_hbm, x_ref), (label_hbm, label_ref), (core_hbm, core_ref)))
    ]
    for copy in copies:
        copy.start()
    for copy in copies:
        copy.wait()
    x = x_ref[...]
    out_ref[0:LANES, :] = x
    xf = x.astype(F32)
    square = xf * xf
    high = square.astype(BF16)
    low = (square - high.astype(F32)).astype(BF16)
    ones = jnp.ones((META, LANES), BF16)
    norm = lax.dot_general(ones, high, NT, preferred_element_type=F32)
    norm = norm + lax.dot_general(ones, low, NT, preferred_element_type=F32)
    core = jnp.broadcast_to(core_ref[...], (META, LANES))
    label = jnp.broadcast_to(label_ref[...].astype(F32), (META, LANES))
    row = lax.broadcasted_iota(jnp.int32, (META, LANES), 0)
    meta = jnp.zeros((META, LANES), F32)
    for k, part in enumerate((*parts_of(norm), *parts_of(core), label)):
        meta = jnp.where(row == k, part, meta)
    both = jnp.concatenate([meta, jnp.zeros((META, LANES), F32)], axis=0)
    out_ref[LANES:, :] = both.astype(BF16)


def join_kernel(cols, own_ref, other_ref, out_ref):
    core = lax.rem(flat_index(cols), 2)
    out_ref[pl.ds(pl.multiple_of(core * LANES, LANES), LANES), :] = own_ref[0:LANES, :]
    out_ref[pl.ds(pl.multiple_of((1 - core) * LANES, LANES), LANES), :] = other_ref[0:LANES, :]
    own = own_ref[LANES:, :].astype(F32)[0:META]
    other = other_ref[LANES:, :].astype(F32)[0:META]
    even = jnp.concatenate([own, other], axis=0)
    odd = jnp.concatenate([other, own], axis=0)
    out_ref[2 * LANES :, :] = jnp.where(core == 0, even, odd).astype(BF16)


def core_of(m8):
    row = lax.broadcasted_iota(jnp.int32, (META, LANES), 0)
    return jnp.sum(jnp.where((row >= 3) & (row < 6), m8, 0.0), axis=0, keepdims=True)


def features(m8, left):
    row = lax.broadcasted_iota(jnp.int32, (2 * META, LANES), 0)
    label = jnp.broadcast_to(m8[6:7], row.shape).astype(jnp.int32)
    same = jnp.where(row == label, 1.0 if left else SAME, 0.0)
    padded = jnp.concatenate([m8, jnp.zeros((META, LANES), F32)], axis=0)
    if left:
        rest = jnp.where(row < 3, padded, jnp.where(row < 6, 1.0, 0.0))
    else:
        rest = jnp.where(row < 3, 1.0, jnp.where(row < 6, pltpu.roll(padded, 3, 0), 0.0))
    return jnp.concatenate([same, rest], axis=0).astype(BF16)


def put_rows(k, ref, which, xr, fr, core_i):
    x = jnp.where(which == 0, ref[0:LANES, :], ref[LANES : 2 * LANES, :])
    xr[k * LANES : (k + 1) * LANES, :] = (x.astype(F32) * -2.0).astype(BF16)
    meta = ref[2 * LANES :, :].astype(F32)
    m8 = jnp.where(which == 0, meta[0:META], meta[META:])
    fr[:, k * LANES : (k + 1) * LANES] = features(m8, False)
    core_i[0:1, k * LANES : (k + 1) * LANES] = core_of(m8)


def nearest(outs, segments, xr, fr, core_i, t_ref, source_of):
    width = 2 * LANES
    blocks, groups_of = len(outs), (width // 8, 8, LANES)

    def over(segments, body, start):
        base = 0
        for xl, fl, key_ref, offsets in segments:
            if body is first_pass and len(offsets) <= 8:
                s = product(xl[...], fl[...])
                for k in range(len(offsets)):
                    start = body(base, xl, fl, key_ref, offsets, k, start, s[k * width : (k + 1) * width])
                base += len(offsets)
                continue
            step = functools.partial(body, base, xl, fl, key_ref, offsets)
            start = lax.fori_loop(0, len(offsets), step, start, unroll=len(offsets) <= 8)
            base += len(offsets)
        return start

    def product(x, f):
        s = lax.dot_general(x, xr[...], NT, preferred_element_type=F32)
        return s + lax.dot_general(f, fr[...], TN, preferred_element_type=F32)

    def first_pass(base, xl, fl, key_ref, offsets, k, best, s=None):
        at = k * width if s is not None else pl.multiple_of(k * width, width)
        if s is None:
            s = product(xl[pl.ds(at, width), :], fl[:, pl.ds(at, width)])
        key = key_ref[pl.ds(at, width), :]
        out = []
        for r in range(blocks):
            t = jnp.maximum(s[:, r * LANES : (r + 1) * LANES], key)
            t_ref[pl.ds(at + base * width, width), r * LANES : (r + 1) * LANES] = t
            out.append(jnp.minimum(best[r], jnp.min(t.reshape(groups_of), axis=0)))
        return tuple(out)

    start = tuple(jnp.full((8, LANES), jnp.inf, F32) for _ in outs)
    best = over(segments, first_pass, start)

    values, limits = [], []
    for r in range(blocks):
        least = jnp.min(best[r], axis=0, keepdims=True)
        mine = core_i[0:1, r * LANES : (r + 1) * LANES]
        none = least > FAR
        root = root_of(least)
        values.append(jnp.where(none, jnp.inf, jnp.maximum(mine, root)))
        base = jnp.maximum(least, key_of(mine))
        limit = jnp.where(root_of(least + 1.0) == root, least + 1.0, least)
        limit = jnp.where(root_of(least + 2.0) == root, least + 2.0, limit)
        limits.append(jnp.where(none, jnp.inf, jnp.where(least > 2.0**21, limit, base)))

    within = lax.broadcasted_iota(jnp.int32, (8, LANES), 0).astype(F32)

    def second_pass(base, xl, fl, key_ref, offsets, k, place):
        at = pl.multiple_of((base + k) * width, width)
        offset = sum(jnp.where(k == i, o, 0) for i, o in enumerate(offsets))
        here = within + (source_of(offset) * width).astype(F32)
        out = []
        for r in range(blocks):
            t = t_ref[pl.ds(at, width), r * LANES : (r + 1) * LANES].reshape(groups_of)
            found = jnp.full((8, LANES), jnp.inf, F32)
            for g in range(width // 8 - 1, -1, -1):
                found = jnp.where(t[g] <= limits[r], 8.0 * g, found)
            out.append(jnp.minimum(place[r], found + here))
        return tuple(out)

    place = over(segments, second_pass, start)
    for r in range(blocks):
        outs[r][0:1, :] = values[r]
        outs[r][1:2, :] = jnp.min(place[r], axis=0, keepdims=True)


def position(cols, ca):
    me = flat_index(cols)
    chip = lax.div(me, 2)
    return lax.rem(me, 2), lax.div(chip, ca), lax.rem(chip, ca)


def split_of(rb, ca):
    steps = gather_offsets(rb, ca)
    early = [k for k in range((len(steps) + 1) // 2, len(steps)) if not any(o[0] for o in steps[k])]
    late = [k for k in range(len(steps)) if k not in early]
    first = [0, *dict.fromkeys(o[1] for k in early for o in steps[k])]
    second = [*dict.fromkeys(o[1] for k in late for o in steps[k] if not o[0] and o[1] not in first)]
    return early, late, first, second


def put_columns(slot, ref, xl, fl, ck):
    row16 = lax.broadcasted_iota(jnp.int32, (2 * META, LANES), 0)
    xl[slot * 2 * LANES : (slot + 1) * 2 * LANES, :] = ref[0 : 2 * LANES, :]
    meta = ref[2 * LANES :, :].astype(F32)
    for h in range(2):
        m8 = meta[h * META : (h + 1) * META]
        at = (2 * slot + h) * LANES
        fl[:, at : at + LANES] = features(m8, True)
        key = jnp.broadcast_to(key_of(core_of(m8)), (2 * META, LANES))
        p0, p1, p2 = parts_of(key)
        ck[:, at : at + LANES] = jnp.where(
            row16 == 0, p0, jnp.where(row16 == 1, p1, jnp.where(row16 == 2, p2, 0.0))
        ).astype(BF16)


def put_gathered(rb, ca, which, core, got, swapped, offsets, columns, rows=None):
    steps = gather_offsets(rb, ca)
    seen = set()
    for k, first, second in zip(which, got, swapped):
        for side in range(2):
            offset = steps[k][side]
            if offset in seen:
                continue
            seen.add(offset)
            block = jnp.where(core == side, first[...], second[...])
            if offset[0]:
                put_rows(offset[0] - 1, block, 1 - core, *rows)
            elif offset[1] in offsets:
                put_columns(offsets.index(offset[1]), block, *columns)


def spread(ck, key_ref):
    take = jnp.where(lax.broadcasted_iota(jnp.int32, (2 * META, LANES), 0) < 3, 1.0, 0.0).astype(BF16)
    key_ref[...] = lax.dot_general(ck[...], take, TN, preferred_element_type=F32)


def early_kernel(cols, rb, ca, own_ref, *refs):
    early, _, offsets, _ = split_of(rb, ca)
    n = len(early)
    got, swapped, (xl, fl, key_ref, ck) = refs[:n], refs[n : 2 * n], refs[2 * n :]
    core = lax.rem(flat_index(cols), 2)
    put_columns(0, own_ref, xl, fl, ck)
    put_gathered(rb, ca, early, core, got, swapped, offsets, (xl, fl, ck))
    spread(ck, key_ref)


def far_kernel(cols, rb, ca, *refs):
    _, late, first, second = split_of(rb, ca)
    n = len(late)
    ready, refs = refs[:3], refs[3:]
    got, swapped = refs[:n], refs[n : 2 * n]
    xl, fl, key_ref, *outs = refs[2 * n : 3 + 2 * n + rb - 1]
    xr, fr, ck, core_i, t_ref = refs[3 + 2 * n + rb - 1 :]
    core, a, b = position(cols, ca)
    put_gathered(rb, ca, late, core, got, swapped, second, (xl, fl, ck), (xr, fr, core_i))
    spread(ck, key_ref)
    segments = [(*ready, first), (xl, fl, key_ref, second)]
    nearest(outs, segments, xr, fr, core_i, t_ref, lambda o: a * ca + came_from(b, o, ca))


def near_kernel(cols, rb, ca, own_ref, *refs):
    _, _, first, second = split_of(rb, ca)
    out_ref, xr, fr, core_i, t_ref = refs[6:]
    core, a, b = position(cols, ca)
    put_rows(0, own_ref, core, xr, fr, core_i)
    segments = [(*refs[:3], first), (*refs[3:6], second)]
    nearest([out_ref], segments, xr, fr, core_i, t_ref, lambda o: a * ca + came_from(b, o, ca))


def merge_kernel(*refs):
    ins, (value_ref, place_ref) = refs[:-2], refs[-2:]
    value, place = ins[0][0:1, :], ins[0][1:2, :]
    for ref in ins[1:]:
        v, p = ref[0:1, :], ref[1:2, :]
        take = (v < value) | ((v == value) & (p < place))
        value, place = jnp.where(take, v, value), jnp.where(take, p, place)
    value_ref[...] = value
    place_ref[...] = place.astype(jnp.int32)


def shards(rows, cols, points, labels, core):
    count = points.shape[0]
    devices = rows * cols
    chips = devices // 2
    rb = 1
    while rb * rb * 8 <= chips:
        rb *= 2
    ca = chips // rb
    axes = ("row", "col")
    vmem = pl.BlockSpec(memory_space=pltpu.VMEM)

    def call(kernel, shapes, *args, scratch=(), grant=4 << 20, space=pltpu.VMEM):
        single = not isinstance(shapes, (tuple, list))
        return pl.pallas_call(
            kernel,
            out_shape=shapes,
            in_specs=[pl.BlockSpec(memory_space=space)] * len(args),
            out_specs=vmem if single else [vmem] * len(shapes),
            scratch_shapes=list(scratch),
            compiler_params=pltpu.CompilerParams(vmem_limit_bytes=grant),
        )(*args)

    def swap(x):
        return lax.ppermute(x, axes, [(d, d ^ 1) for d in range(devices)])

    def chip_to(chip, offset):
        a, b = divmod(chip, ca)
        return moved(a, offset[0], rb) * ca + moved(b, offset[1], ca)

    inputs = (points, labels.reshape(1, count), core.reshape(1, count))
    own = call(
        pack_kernel,
        jax.ShapeDtypeStruct((count + 2 * META, LANES), BF16),
        *(pltpu.with_memory_space_constraint(x, pltpu.HBM) for x in inputs),
        space=pltpu.HBM,
        scratch=[pltpu.VMEM(x.shape, x.dtype) for x in inputs] + [pltpu.SemaphoreType.DMA((len(inputs),))],
    )
    block = call(
        functools.partial(join_kernel, cols),
        jax.ShapeDtypeStruct((2 * count + 2 * META, LANES), BF16),
        own,
        swap(own),
    )

    got = []
    for offsets in gather_offsets(rb, ca):
        pairs = [(2 * q + side, 2 * chip_to(q, offsets[side]) + side) for q in range(chips) for side in range(2)]
        got.append(lax.ppermute(block, axes, pairs))
    swapped = [swap(x) for x in got]

    wide, far = 2 * count * ca, count * (rb - 1)
    early, late, first_offsets, second_offsets = split_of(rb, ca)

    def held(offsets):
        n = 2 * count * len(offsets)
        shapes = (((n, LANES), BF16), ((32, n), BF16), ((n, LANES), F32))
        return [jax.ShapeDtypeStruct(*x) for x in shapes], pltpu.VMEM((2 * META, n), BF16)

    def row_scratch(n):
        return [pltpu.VMEM((n, LANES), BF16), pltpu.VMEM((32, n), BF16)], [pltpu.VMEM((8, n), F32), pltpu.VMEM((wide, n), F32)]

    shapes, ck = held(first_offsets)
    ready = call(
        functools.partial(early_kernel, cols, rb, ca),
        shapes,
        block,
        *(got[k] for k in early),
        *(swapped[k] for k in early),
        scratch=[ck],
    )
    found = jax.ShapeDtypeStruct((8, LANES), F32)
    shapes, ck = held(second_offsets)
    first, last = row_scratch(far)
    results = call(
        functools.partial(far_kernel, cols, rb, ca),
        [*shapes, *[found] * (rb - 1)],
        *ready,
        *(got[k] for k in late),
        *(swapped[k] for k in late),
        scratch=[*first, ck, *last],
        grant=(6 << 20) + 2 * wide * far * 4,
    )
    columns, partial = [*ready, *results[:3]], results[3:]
    back = []
    for k in range(1, rb):
        pairs = [(d, 2 * chip_to(d // 2, (k, 0)) + 1 - d % 2) for d in range(devices)]
        back.append(lax.ppermute(partial[k - 1], axes, pairs))
    first, last = row_scratch(count)
    own_found = call(
        functools.partial(near_kernel, cols, rb, ca),
        found,
        block,
        *columns,
        scratch=[*first, *last],
        grant=(6 << 20) + 2 * wide * count * 4,
    )
    back.insert(0, own_found)
    value, place = call(
        merge_kernel,
        [jax.ShapeDtypeStruct((1, count), F32), jax.ShapeDtypeStruct((1, count), jnp.int32)],
        *back,
    )
    return value.reshape(count), place.reshape(count)


def solution(mesh):
    rows, cols = mesh.shape["row"], mesh.shape["col"]
    return jax.shard_map(
        functools.partial(shards, rows, cols),
        mesh=mesh,
        in_specs=(P(("row", "col"), None), P(("row", "col")), P(("row", "col"))),
        out_specs=(P(("row", "col")), P(("row", "col"))),
        check_vma=False,
    )
```
